128 devices in a mesh: batch: 8 (over x, core), item: 16 (over z, y).
Axes of the slice: x: 4, y: 4, z: 4, core: 2. Of those that a mesh axis runs over, the one named last changes fastest.
Arguments:
- user_vectors: bfloat16 [32768, 512], P(('batch', 'item')), may hold values from -6 to 6
- item_table: bfloat16 [524288, 512], P(('batch', 'item')), may hold values from -0.25 to 0.25
- tower_weight: bfloat16 [512, 512], replicated, may hold values from -3 to 3
- item_owner: int32 [32768, 1], P(('batch', 'item')), may hold values from 0 to 127; in each aligned block of 256 rows (0 to 255, 256 to 511, ...) at most 4 rows name the same one
- item_row: int32 [32768], P(('batch', 'item')), may hold values from 0 to 4095
Outputs:
- table_grad: bfloat16 [524288, 512], P(('batch', 'item'))
- weight_grad: float32 [512, 512], P(('batch', 'item'))
The draws below stay inside these ranges and needn't reach their ends.
Inputs may be any that keep to these rules, and one draw needn't show every extreme that they name: `item_owner`: within the rows of one device (aligned blocks of 256 rows) no owner is named by more than 4 rows, a bound that some block reaches.
All inputs are finite; a program needn't handle non-finite values.
Results may differ from the reference program's by a relative error of at most 0.0075.
Values may be sent and summed in bfloat16 or wider, within the bound.
A program may use at most 64 MiB of HBM per device.

```python
import math
import jax
import jax.numpy as jnp
import numpy as np
from jax import lax

D = 512
B_DEV = 256
ROWS_DEV = 4096
TOTAL = 32768
ITEMS = 524288
OWNERS = 128
CAP = 4
GROUP = 2048
N_BATCH = 8
N_ITEM = 16


def place_ends(entries, rng, low, top_value):
    shape = entries.shape
    spot = [jax.random.randint(jax.random.fold_in(rng, axis), (), 0, shape[axis]) for axis in range(len(shape))]
    entries = entries.at[tuple(spot)].set(low)
    longest = shape.index(max(shape))
    spot[longest] = (spot[longest] + 1) % shape[longest]
    return entries.at[tuple(spot)].set(top_value)


def block_scale(key, dims, shards, least, largest):
    level, own = 1.0, jax.random.fold_in(key, 6)
    for dim, blocks in shards:
        heights = jnp.exp(jax.random.uniform(jax.random.fold_in(own, dim), (blocks,), jnp.float32, least / len(shards), largest / len(shards)))
        level = level * jnp.repeat(heights, dims[dim] // blocks).reshape([-1 if axis == dim else 1 for axis in range(len(dims))])
    return level


def deal_out(key, own, number, rows, number_of, top, limit, slope):
    ranking = jax.random.permutation(key, number_of)
    crowded, ordinary = shares(number_of, rows * top, limit, slope, True), shares(number_of, rows * top, limit, slope, False)
    places = jnp.arange(number_of)

    def named(tallies, turn):
        used = int((tallies > 0).sum())
        fixed = max(1, used // 4)
        shifted = fixed + (places - fixed + turn * (used - fixed)) % max(1, number_of - fixed)
        return jnp.zeros((number_of,), jnp.int32).at[ranking[jnp.where(places < fixed, places, shifted)]].set(jnp.asarray(tallies, jnp.int32))

    tallies = jnp.where(number % 4 == 0, named(crowded, number // 4), named(ordinary, number - number // 4 - 1))
    mixed = jax.random.permutation(jax.random.fold_in(own, 3), number_of)
    giver, taker = mixed[0:number_of // 2 * 2:2], mixed[1:number_of // 2 * 2:2]
    margin = jnp.minimum(tallies[giver] - 1, limit - tallies[taker]) // 2
    margin = jnp.where((giver == ranking[0]) | (taker == ranking[0]) | (tallies[taker] == 0), 0, jnp.maximum(margin, 0))
    shifted = jax.random.randint(jax.random.fold_in(own, 4), (number_of // 2,), 0, 1 << 20) % (margin + 1)
    tallies = tallies.at[giver].add(-shifted).at[taker].add(shifted)
    labels = jnp.searchsorted(jnp.cumsum(tallies), jnp.arange(rows * top), side="right").astype(jnp.int32)
    listing = labels.reshape(top, rows).T
    listing = listing[jax.random.permutation(jax.random.fold_in(own, 1), rows)]
    turn = jax.random.randint(jax.random.fold_in(own, 2), (rows, 1), 0, top)
    return jnp.take_along_axis(listing, (jnp.arange(top)[None, :] + turn) % top, axis=1)


def shares(number_of, total, bound, lean, full):
    portions = [(1 << 20) // math.isqrt(grade ** lean) + 1 for grade in range(1, number_of + 1)]
    largest = bound if full else min(bound, max(-(-total // number_of), total * portions[0] // sum(portions)))
    least = 1 if total - largest >= number_of - 1 else 0
    holding, spare = [largest] + [least] * (number_of - 1), total - largest - least * (number_of - 1)
    while spare > 0:
        free = [i for i in range(1, number_of) if holding[i] < largest] or [i for i in range(1, number_of) if holding[i] < bound]
        whole, left = sum([portions[i] for i in free]), spare
        for i in free:
            addition = min(bound - holding[i], max(1, left * portions[i] // whole), spare)
            holding[i] = holding[i] + addition
            spare = spare - addition
    return np.array(holding)


def bell_draw(own_key, shape, width, bound, cuts=(), kind=jnp.bfloat16):
    drawn = jax.random.normal(own_key, shape, jnp.float32) * width
    if len(cuts) > 0:
        drawn = block_scale(own_key, shape, cuts, -0.22, 0.18) * drawn
    return jnp.clip(drawn, min=-bound, max=bound).astype(kind)


def setup_inputs(seed: int = 0) -> dict:
    keys = jax.random.split(jax.random.key(seed), 6)
    user_vectors = bell_draw(keys[0], (TOTAL, D), 1.0, 6.0, ((0, 128),))
    item_table = bell_draw(keys[1], (ITEMS, D), D ** -0.5, 0.25, ((0, 128),))
    tower_weight = bell_draw(keys[2], (D, D), (D // 128) ** -0.5, 3.0)
    item_owner_keys = jax.random.split(jax.random.fold_in(keys[3], 1), TOTAL // B_DEV)
    item_owner_turns = jax.random.permutation(jax.random.fold_in(keys[3], 3), TOTAL // B_DEV)
    item_owner = jax.vmap(lambda own, number: deal_out(jax.random.fold_in(keys[3], 2), own, number, B_DEV, OWNERS, 1, CAP, 2))(item_owner_keys, item_owner_turns).reshape((TOTAL, 1))
    item_row = place_ends(jax.random.randint(keys[4], (TOTAL,), 0, ROWS_DEV), jax.random.fold_in(keys[4], 1), 0, ROWS_DEV - 1).astype(jnp.int32)
    return {"user_vectors": user_vectors, "item_table": item_table, "tower_weight": tower_weight, "item_owner": item_owner, "item_row": item_row}


epsilon = 1e-06
score_scale = 60.0
cauchy_scale = 4.0

def group_grad(pair):
    item_vec, user_unit = pair
    score = jnp.dot(item_vec, user_unit.T, preferred_element_type=jnp.float32) * score_scale
    expo = jnp.exp(score)
    total = lax.optimization_barrier(jnp.sum(expo, axis=1))
    mixed = jnp.dot(expo.astype(jnp.bfloat16), user_unit, preferred_element_type=jnp.float32)
    user_f = user_unit.astype(jnp.float32)
    positive = lax.optimization_barrier(jnp.sum(item_vec.astype(jnp.float32) * user_f, axis=1)) * score_scale
    xent = jnp.log(total) - positive
    cweight = 1.0 / (1.0 + xent / cauchy_scale)
    return cweight[:, None] * score_scale * (mixed / total[:, None] - user_f)

def regroup(values):
    return values.reshape(N_BATCH, N_ITEM, B_DEV, D).transpose(1, 0, 2, 3).reshape(N_ITEM, GROUP, D)

def reference(user_vectors, item_table, tower_weight, item_owner, item_row):
    item_id = (item_owner[:, 0] * ROWS_DEV + item_row).astype(jnp.int32)
    embed = item_table[item_id]
    hidden = jnp.dot(embed, tower_weight, preferred_element_type=jnp.float32)
    rscale = lax.rsqrt(lax.optimization_barrier(jnp.mean(hidden * hidden, axis=1, keepdims=True)) + epsilon)
    item_vec = (hidden * rscale / jnp.sqrt(jnp.float32(D))).astype(jnp.bfloat16)
    user_f = user_vectors.astype(jnp.float32)
    user_unit = (user_f * lax.rsqrt(lax.optimization_barrier(jnp.mean(user_f * user_f, axis=1, keepdims=True)) + epsilon) / jnp.sqrt(jnp.float32(D))).astype(jnp.bfloat16)
    dvec = lax.map(group_grad, (regroup(item_vec), regroup(user_unit)))
    dvec = dvec.reshape(N_ITEM, N_BATCH, B_DEV, D).transpose(1, 0, 2, 3).reshape(TOTAL, D)
    inner = lax.optimization_barrier(jnp.sum(hidden * dvec, axis=1, keepdims=True))
    dhidden = (rscale / jnp.sqrt(jnp.float32(D)) * (dvec - hidden * rscale * rscale * inner / D)).astype(jnp.bfloat16)
    weight_grad = jnp.dot(embed.T, dhidden, preferred_element_type=jnp.float32)
    drow = jnp.dot(dhidden, tower_weight.T, preferred_element_type=jnp.float32)
    table_grad = jnp.zeros((ITEMS, D), jnp.float32).at[item_id].add(drow).astype(jnp.bfloat16)
    return (table_grad, weight_grad)
```

```python
import jax
import jax.numpy as jnp
from jax import lax
from jax.sharding import PartitionSpec as P

epsilon = 1e-06
score_scale = 60.0
cauchy_scale = 4.0


def local(user_vectors, item_table, tower_weight, item_owner, item_row):
    b_dev, width = user_vectors.shape
    n_batch = lax.axis_size("batch")
    n_item = lax.axis_size("item")
    devices = n_batch * n_item
    slots = 2 * b_dev // devices
    owner = item_owner[:, 0]
    onehot = (owner[:, None] == jnp.arange(devices, dtype=jnp.int32)[None, :]).astype(jnp.int32)
    rank = jnp.sum(jnp.cumsum(onehot, axis=0) * onehot, axis=1) - 1
    place = owner * slots + rank
    request = (
        jnp.zeros((devices * slots,), jnp.int32).at[place].set(item_row).reshape(devices, slots)
    )
    asked = lax.all_to_all(request, ("batch", "item"), split_axis=0, concat_axis=0, tiled=True)
    found = item_table[asked]
    back = lax.all_to_all(found, ("batch", "item"), split_axis=0, concat_axis=0, tiled=True)
    fetched, asked = (back, asked)
    embed = fetched.reshape(devices * slots, width)[place]
    hidden = jnp.dot(embed, tower_weight, preferred_element_type=jnp.float32)
    rscale = lax.rsqrt(jnp.mean(hidden * hidden, axis=1, keepdims=True) + epsilon)
    item_vec = (hidden * rscale / jnp.sqrt(jnp.float32(width))).astype(jnp.bfloat16)
    user_f = user_vectors.astype(jnp.float32)
    user_unit = (
        user_f
        * lax.rsqrt(jnp.mean(user_f * user_f, axis=1, keepdims=True) + epsilon)
        / jnp.sqrt(jnp.float32(width))
    ).astype(jnp.bfloat16)
    piece = lax.all_gather(user_unit, "batch", axis=0, tiled=True)
    score = (
        lax.dot_general(
            item_vec, piece, (((1,), (1,)), ((), ())), preferred_element_type=jnp.float32
        )
        * score_scale
    )
    expo = jnp.exp(score)
    partial_mix = jnp.dot(expo.astype(jnp.bfloat16), piece, preferred_element_type=jnp.float32)
    total = jnp.sum(expo, axis=1)
    unit_f = user_unit.astype(jnp.float32)
    positive = jnp.sum(item_vec.astype(jnp.float32) * unit_f, axis=1) * score_scale
    xent = jnp.log(total) - positive
    cweight = 1.0 / (1.0 + xent / cauchy_scale)
    dvec = cweight[:, None] * score_scale * (partial_mix / total[:, None] - unit_f)
    inner = jnp.sum(hidden * dvec, axis=1, keepdims=True)
    dhidden = (
        rscale / jnp.sqrt(jnp.float32(width)) * (dvec - hidden * rscale * rscale * inner / width)
    ).astype(jnp.bfloat16)
    share = lax.dot_general(
        embed, dhidden, (((0,), (0,)), ((), ())), preferred_element_type=jnp.float32
    ).astype(jnp.bfloat16)
    shares = lax.all_to_all(
        share.reshape(devices, width // devices, width),
        ("batch", "item"),
        split_axis=0,
        concat_axis=0,
        tiled=True,
    )
    weight_grad = jnp.sum(shares.astype(jnp.float32), axis=0)
    drow = jnp.dot(dhidden, tower_weight.T, preferred_element_type=jnp.float32)
    outgoing = jnp.zeros((devices * slots, width), jnp.float32).at[place].set(drow)
    incoming = lax.all_to_all(
        outgoing.reshape(devices, slots, width).astype(jnp.bfloat16),
        ("batch", "item"),
        split_axis=0,
        concat_axis=0,
        tiled=True,
    ).astype(jnp.float32)
    arrived = incoming.reshape(devices * slots, width)
    table_grad = (
        jnp.zeros((item_table.shape[0], width), jnp.float32).at[asked.reshape(-1)].add(arrived)
    )
    return (table_grad.astype(jnp.bfloat16), weight_grad)


def solution(mesh):
    return jax.shard_map(
        local,
        mesh=mesh,
        in_specs=(
            P(("batch", "item"), None),
            P(("batch", "item"), None),
            P(),
            P(("batch", "item"), None),
            P(("batch", "item")),
        ),
        out_specs=(P(("batch", "item"), None), P(("batch", "item"), None)),
        check_vma=False,
    )
```

```python
import functools

import jax
import jax.numpy as jnp
from jax import lax
from jax.experimental import pallas as pl
from jax.experimental.pallas import tpu as pltpu
from jax.sharding import PartitionSpec as P

epsilon = 1e-06
score_scale = 60.0
cauchy_scale = 4.0

MESH = pl.DeviceIdType.MESH
BF = jnp.bfloat16
F32 = jnp.float32
I32 = jnp.int32
D = 512
BD = 256
ROWS = 4096
SLOTS = 4
NDEV = 128
NCH = 4
CH = NDEV // NCH
CS = CH * SLOTS


def nt(a, b):
    return lax.dot_general(a, b, (((1,), (1,)), ((), ())), preferred_element_type=F32)


def tn(a, b):
    return lax.dot_general(a, b, (((0,), (0,)), ((), ())), preferred_element_type=F32)


def step_kernel(
    user_ref,
    table_ref,
    w_ref,
    owner_ref,
    row_ref,
    drow_out,
    askrow_out,
    wg_out,
    table_v,
    req,
    t1,
    asked,
    cols,
    reply,
    emb,
    embn,
    drs,
    dr,
    ug,
    us,
    valid,
    dhid,
    onehot,
    wgs,
    wgr,
    wg2,
    wg3,
    tsem,
    ag_s,
    ag_r,
    rq_s,
    rq_r,
    rp_s,
    rp_r,
    gr_s,
    gr_r,
    wg_s,
    wg_r,
):
    b, it = lax.axis_index("batch"), lax.axis_index("item")
    x, c = b // 2, lax.rem(b, 2)
    z, y = it // 4, lax.rem(it, 4)

    def at(xi, ga, ze, et):
        px, pc = lax.rem(x + xi, 4), lax.rem(c + ga, 2)
        pz, py = lax.rem(z + ze, 4), lax.rem(y + et, 4)
        return (px * 2 + pc, pz * 4 + py)

    def send(src, dst, ss, rs, to):
        cp = pltpu.make_async_remote_copy(
            src_ref=src, dst_ref=dst, send_sem=ss, recv_sem=rs, device_id=to, device_id_type=MESH
        )
        cp.start()

    def drain(ref, sem):
        pltpu.make_async_copy(ref, ref, sem).wait()

    table_cp = pltpu.make_async_copy(table_ref, table_v, tsem)
    table_cp.start()

    bar = pltpu.get_barrier_semaphore()
    for k in range(1, 8):
        pl.semaphore_signal(bar, inc=1, device_id=at(k // 2, k % 2, 0, 0), device_id_type=MESH)
    for k in range(1, 16):
        pl.semaphore_signal(bar, inc=1, device_id=at(0, 0, k // 4, k % 4), device_id_type=MESH)

    uf = user_ref[...].astype(F32)
    uu = (
        uf
        * lax.rsqrt(jnp.mean(uf * uf, axis=1, keepdims=True) + epsilon)
        / jnp.sqrt(F32(D))
    ).astype(BF)
    ug[0] = uu

    ow = owner_ref[...]
    ox, oc = ow // 32, (ow // 16) % 2
    oz, oy = (ow // 4) % 4, ow % 4
    rx, rc = (ox - x + 4) % 4, (oc - c + 2) % 2
    rz, ry = (oz - z + 4) % 4, (oy - y + 4) % 4
    pos = (ry * 8 + rx * 2 + rc) * 4 + rz
    oh = pos == lax.broadcasted_iota(I32, (NDEV, BD), 0)
    ohf = jnp.where(oh, F32(1), F32(0))
    upper = jnp.where(
        lax.broadcasted_iota(I32, (BD, BD), 0) < lax.broadcasted_iota(I32, (BD, BD), 1),
        F32(1),
        F32(0),
    ).astype(BF)
    before = jnp.dot(ohf.astype(BF), upper, preferred_element_type=F32)
    rank = jnp.sum(before * ohf, axis=0, keepdims=True)
    place = pos * SLOTS + rank.astype(I32)
    pt = place == lax.broadcasted_iota(I32, (NDEV * SLOTS, BD), 0)
    ptf = jnp.where(pt, F32(1), F32(0))
    want = jnp.sum(jnp.where(pt, row_ref[...].astype(F32), F32(0)), axis=1, keepdims=True)
    req[...] = jnp.broadcast_to(want.astype(I32), (NDEV * SLOTS, 128)).reshape(
        NCH, 8, 4, SLOTS, 128
    )
    valid[...] = jnp.broadcast_to(jnp.sum(ptf, axis=1, keepdims=True), (NDEV * SLOTS, 128))

    pl.semaphore_wait(bar, 22)

    for k in range(1, 8):
        send(req.at[:, k], t1.at[:, k], rq_s.at[0], rq_r.at[0], at(k // 2, k % 2, 0, 0))
    send(ug.at[0], ug.at[1], ag_s.at[0], ag_r.at[0], at(0, 1, 0, 0))
    send(ug.at[0], ug.at[2], ag_s.at[1], ag_r.at[1], at(1, 0, 0, 0))
    send(ug.at[0], ug.at[4], ag_s.at[2], ag_r.at[2], at(3, 0, 0, 0))
    t1[:, 0] = req[:, 0]
    us[...] = jnp.dot(ptf.astype(BF), ug[0], preferred_element_type=F32).astype(BF)
    drain(t1.at[:, pl.ds(1, 7)], rq_r.at[0])
    for k in range(1, 16):
        ze, et = k // 4, k % 4
        send(t1.at[et, :, ze], asked.at[et, :, ze], rq_s.at[1], rq_r.at[1], at(0, 0, ze, et))
    asked[0, :, 0] = t1[0, :, 0]
    table_cp.wait()
    drain(req.at[:, pl.ds(1, 7)], rq_s.at[0])
    h = BD // 2
    drain(ug.at[2], ag_r.at[1])
    send(ug.at[2, pl.ds(0, h)], ug.at[6, pl.ds(0, h)], ag_s.at[3], ag_r.at[3], at(1, 0, 0, 0))
    send(ug.at[2], ug.at[3], ag_s.at[5], ag_r.at[5], at(0, 1, 0, 0))
    drain(ug.at[4], ag_r.at[2])
    send(ug.at[4, pl.ds(h, h)], ug.at[6, pl.ds(h, h)], ag_s.at[4], ag_r.at[4], at(3, 0, 0, 0))
    send(ug.at[4], ug.at[5], ag_s.at[6], ag_r.at[6], at(0, 1, 0, 0))

    hop2 = cols.at[pl.ds(0, 15 * 8 * SLOTS)]
    drain(hop2, rq_r.at[1])

    cols[...] = asked[...].reshape(NDEV * SLOTS, 128)
    eye = lax.broadcasted_iota(I32, (128, 128), 0) == lax.broadcasted_iota(I32, (128, 128), 1)
    for g in range(NCH):
        a = cols[g * CS : (g + 1) * CS, :]
        askrow_out[:, g * CS : (g + 1) * CS] = jnp.broadcast_to(
            jnp.sum(jnp.where(eye, a, 0), axis=0, keepdims=True), (8, CS)
        )
        for j in range(ROWS // 128):
            hit = a == lax.broadcasted_iota(I32, (CS, 128), 1) + j * 128
            onehot[g * CS : (g + 1) * CS, j * 128 : (j + 1) * 128] = jnp.where(
                hit, F32(1), F32(0)
            ).astype(BF)
        found = jnp.dot(
            onehot[g * CS : (g + 1) * CS, :], table_v[...], preferred_element_type=F32
        )
        reply[g * CH : (g + 1) * CH] = found.astype(BF).reshape(CH, SLOTS, D)

        def back(i, _):
            beta, ze = lax.rem(i // 4, 8), lax.rem(i, 4)
            to = at(4 - beta // 2, lax.rem(beta, 2), 4 - ze, 4 - g)
            send(reply.at[pl.ds(i, 1)], emb.at[pl.ds(i, 1)], rp_s, rp_r.at[g], to)
            return 0

        lax.fori_loop(max(1, g * CH), (g + 1) * CH, back, 0)
        if g == 0:
            emb[0] = reply[0]

    drain(ug.at[6, pl.ds(0, h)], ag_r.at[3])
    drain(ug.at[6, pl.ds(h, h)], ag_r.at[4])
    send(ug.at[6], ug.at[7], ag_s.at[7], ag_r.at[7], at(0, 1, 0, 0))
    drain(ug.at[1], ag_r.at[0])
    drain(ug.at[3], ag_r.at[5])
    drain(ug.at[5], ag_r.at[6])
    drain(ug.at[7], ag_r.at[7])
    root = jnp.sqrt(F32(D))
    for g in range(NCH):
        lo = 1 if g == 0 else g * CH
        drain(emb.at[pl.ds(lo, (g + 1) * CH - lo)], rp_r.at[g])
        sl = slice(g * CS, (g + 1) * CS)
        e = emb[g * CH : (g + 1) * CH].reshape(CS, D)
        embn[sl, :] = e
        hid = jnp.dot(e, w_ref[...], preferred_element_type=F32)
        rs = lax.rsqrt(jnp.mean(hid * hid, axis=1, keepdims=True) + epsilon)
        iv = (hid * rs / root).astype(BF)
        tot = jnp.zeros((CS, 1), F32)
        mix = jnp.zeros((CS, D), F32)
        for k in range(8):
            ex = jnp.exp(nt(iv, ug[k]) * score_scale)
            tot = tot + jnp.sum(ex, axis=1, keepdims=True)
            mix = mix + jnp.dot(ex.astype(BF), ug[k], preferred_element_type=F32)
        uf2 = us[sl, :].astype(F32)
        positive = jnp.sum(iv.astype(F32) * uf2, axis=1, keepdims=True) * score_scale
        xent = jnp.log(tot) - positive
        cw = 1.0 / (1.0 + xent / cauchy_scale)
        dvec = cw * score_scale * (mix / tot - uf2)
        inner = jnp.sum(hid * dvec, axis=1, keepdims=True)
        dh = rs / root * (dvec - hid * rs * rs * inner / D)
        dh = jnp.where(valid[sl, 0:1] > 0.5, dh, F32(0)).astype(BF)
        dhid[sl, :] = dh
        drs[g * CH : (g + 1) * CH] = nt(dh, w_ref[...]).astype(BF).reshape(CH, SLOTS, D)

        def out(i, _):
            beta, ze = lax.rem(i // 4, 8), lax.rem(i, 4)
            to = at(beta // 2, lax.rem(beta, 2), ze, g)
            send(drs.at[pl.ds(i, 1)], dr.at[pl.ds(i, 1)], gr_s, gr_r, to)
            return 0

        lax.fori_loop(lo, (g + 1) * CH, out, 0)
    dr[0] = drs[0]

    wgs[...] = tn(embn[...], dhid[...]).astype(BF).reshape(8, 64, D)
    for k in range(4):
        send(wgs.at[k * 2 + 1 - c], wgr.at[k], wg_s.at[0], wg_r.at[0], at(0, 1, 0, 0))
    drain(wgr, wg_r.at[0])
    for k in range(4):
        both = wgs[k * 2 + c].astype(F32) + wgr[k].astype(F32)
        wg2[k * 16 : (k + 1) * 16] = both.astype(BF).reshape(16, 4, D)

    def spread(j, _):
        xi, ze, et = j // 16, lax.rem(j // 4, 4), lax.rem(j, 4)
        to = at(xi, 0, ze, et)
        mine = lax.rem(x + xi, 4) * 16 + lax.rem(z + ze, 4) * 4 + lax.rem(y + et, 4)
        send(wg2.at[pl.ds(mine, 1)], wg3.at[pl.ds(j, 1)], wg_s.at[1], wg_r.at[1], to)
        return 0

    lax.fori_loop(1, 64, spread, 0)
    wg3[0] = wg2[x * 16 + z * 4 + y]

    drain(dr.at[pl.ds(1, NDEV - 1)], gr_r)
    drow_out[...] = dr[...].reshape(NDEV * SLOTS, D)

    drain(wg3.at[pl.ds(1, 63)], wg_r.at[1])
    wg_out[...] = jnp.sum(wg3[...].astype(F32), axis=0)

    drain(hop2, rq_s.at[1])
    for k in range(3):
        drain(ug.at[0], ag_s.at[k])
    drain(ug.at[2, pl.ds(0, h)], ag_s.at[3])
    drain(ug.at[4, pl.ds(h, h)], ag_s.at[4])
    drain(ug.at[2], ag_s.at[5])
    drain(ug.at[4], ag_s.at[6])
    drain(ug.at[6], ag_s.at[7])
    drain(reply.at[pl.ds(1, NDEV - 1)], rp_s)
    drain(drs.at[pl.ds(1, NDEV - 1)], gr_s)
    drain(wgr, wg_s.at[0])
    drain(wg2.at[pl.ds(1, 63)], wg_s.at[1])


def table_kernel(ask_ref, drow_ref, out_ref):
    n = out_ref.shape[0]
    base = pl.program_id(0) * n
    hit = ask_ref[0:1, :] == lax.broadcasted_iota(I32, (n, NDEV * SLOTS), 0) + base
    mat = jnp.where(hit, F32(1), F32(0)).astype(BF)
    out_ref[...] = jnp.dot(mat, drow_ref[...], preferred_element_type=F32).astype(BF)


def local(user_vectors, item_table, tower_weight, item_owner, item_row):
    dma = pltpu.SemaphoreType.DMA
    vm = pl.BlockSpec(memory_space=pltpu.VMEM)
    n = NDEV * SLOTS
    scratch = [
        pltpu.VMEM((ROWS, D), BF),
        pltpu.VMEM((4, 8, 4, SLOTS, 128), I32),
        pltpu.VMEM((4, 8, 4, SLOTS, 128), I32),
        pltpu.VMEM((4, 8, 4, SLOTS, 128), I32),
        pltpu.VMEM((n, 128), I32),
        pltpu.VMEM((NDEV, SLOTS, D), BF),
        pltpu.VMEM((NDEV, SLOTS, D), BF),
        pltpu.VMEM((n, D), BF),
        pltpu.VMEM((NDEV, SLOTS, D), BF),
        pltpu.VMEM((NDEV, SLOTS, D), BF),
        pltpu.VMEM((8, BD, D), BF),
        pltpu.VMEM((n, D), BF),
        pltpu.VMEM((n, 128), F32),
        pltpu.VMEM((n, D), BF),
        pltpu.VMEM((n, ROWS), BF),
        pltpu.VMEM((8, 64, D), BF),
        pltpu.VMEM((4, 64, D), BF),
        pltpu.VMEM((64, 4, D), BF),
        pltpu.VMEM((64, 4, D), BF),
        dma,
        dma((8,)),
        dma((8,)),
        dma((2,)),
        dma((2,)),
        dma,
        dma((NCH,)),
        dma,
        dma,
        dma((2,)),
        dma((2,)),
    ]
    drow, ask, wgrad = pl.pallas_call(
        step_kernel,
        out_shape=(
            jax.ShapeDtypeStruct((n, D), BF),
            jax.ShapeDtypeStruct((8, n), I32),
            jax.ShapeDtypeStruct((4, D), F32),
        ),
        in_specs=[vm, pl.BlockSpec(memory_space=pl.ANY), vm, vm, vm],
        out_specs=(vm, vm, vm),
        scratch_shapes=scratch,
        compiler_params=pltpu.CompilerParams(
            collective_id=0, has_side_effects=True, vmem_limit_bytes=60 * 1024 * 1024
        ),
    )(user_vectors, item_table, tower_weight, item_owner.reshape(1, BD), item_row.reshape(1, BD))
    blk = 512
    tgrad = pl.pallas_call(
        table_kernel,
        grid=(ROWS // blk,),
        out_shape=jax.ShapeDtypeStruct((ROWS, D), BF),
        in_specs=[
            pl.BlockSpec((8, n), lambda i: (0, 0)),
            pl.BlockSpec((n, D), lambda i: (0, 0)),
        ],
        out_specs=pl.BlockSpec((blk, D), lambda i: (i, 0)),
    )(ask, drow)
    return tgrad, wgrad


def solution(mesh):
    return jax.shard_map(
        local,
        mesh=mesh,
        in_specs=(
            P(("batch", "item"), None),
            P(("batch", "item"), None),
            P(),
            P(("batch", "item"), None),
            P(("batch", "item")),
        ),
        out_specs=(P(("batch", "item"), None), P(("batch", "item"), None)),
        check_vma=False,
    )
```

```python
import functools

import jax
import jax.numpy as jnp
from jax import lax
from jax.experimental import pallas as pl
from jax.experimental.pallas import tpu as pltpu
from jax.sharding import PartitionSpec as P

epsilon = 1e-06
score_scale = 60.0
cauchy_scale = 4.0

MESH = pl.DeviceIdType.MESH
BF = jnp.bfloat16
F32 = jnp.float32
I32 = jnp.int32
D = 512
BD = 256
ROWS = 4096
SLOTS = 4
NDEV = 128
NCH = 4
CH = NDEV // NCH
CS = CH * SLOTS


def nt(a, b):
    return lax.dot_general(a, b, (((1,), (1,)), ((), ())), preferred_element_type=F32)


def tn(a, b):
    return lax.dot_general(a, b, (((0,), (0,)), ((), ())), preferred_element_type=F32)


def step_kernel(
    user_ref,
    table_ref,
    w_ref,
    owner_ref,
    row_ref,
    drow_out,
    askrow_out,
    wg_out,
    user_v,
    w_v,
    owner_v,
    row_v,
    table_v,
    req,
    t1,
    asked,
    cols,
    reply,
    emb,
    drs,
    dr,
    ug,
    back,
    forth,
    exb,
    onehot,
    wgs,
    wgr,
    wg2,
    wg3,
    in_s,
    ag_s,
    ag_r,
    rq_s,
    rq_r,
    rp_s,
    rp_r,
    gr_s,
    gr_r,
    wg_s,
    wg_r,
):
    b, it = lax.axis_index("batch"), lax.axis_index("item")
    x, c = b // 2, lax.rem(b, 2)
    z, y = it // 4, lax.rem(it, 4)
    xs = [lax.rem(x + k, 4) * 2 for k in range(4)]
    cs = [lax.rem(c + k, 2) for k in range(2)]
    zs = [lax.rem(z + k, 4) * 4 for k in range(4)]
    ys = [lax.rem(y + k, 4) for k in range(4)]

    def at(xi, ga, ze, et):
        return (xs[xi % 4] + cs[ga % 2], zs[ze % 4] + ys[et % 4])

    def split(i):
        return (i % 8) // 2, i % 2, (i // 8) % 4, i // 32

    def send(src, dst, ss, rs, to):
        pltpu.make_async_remote_copy(
            src_ref=src, dst_ref=dst, send_sem=ss, recv_sem=rs, device_id=to, device_id_type=MESH
        ).start()

    def drain(ref, sem):
        pltpu.make_async_copy(ref, ref, sem).wait()

    fetch = [
        pltpu.make_async_copy(src, dst, in_s.at[k])
        for k, (src, dst) in enumerate(
            [
                (owner_ref, owner_v),
                (row_ref, row_v),
                (user_ref, user_v),
                (w_ref, w_v),
                (table_ref, table_v),
            ]
        )
    ]
    for cp in fetch:
        cp.start()
    bar = pltpu.get_barrier_semaphore()
    for k in range(1, 8):
        pl.semaphore_signal(bar, inc=1, device_id=at(k // 2, k % 2, 0, 0), device_id_type=MESH)
    for k in range(1, 16):
        pl.semaphore_signal(bar, inc=1, device_id=at(0, 0, k % 4, k // 4), device_id_type=MESH)

    fetch[0].wait()
    fetch[1].wait()
    ow = owner_v[...]
    ox, oc = ow // 32, (ow // 16) % 2
    oz, oy = (ow // 4) % 4, ow % 4
    rx, rc = (ox - x + 4) % 4, (oc - c + 2) % 2
    rz, ry = (oz - z + 4) % 4, (oy - y + 4) % 4
    beta = rx * 2 + rc
    plane = ry * 4 + rz
    pos = plane * 8 + beta
    ohf = jnp.where(pos == lax.broadcasted_iota(I32, (NDEV, BD), 0), F32(1), F32(0))
    upper = jnp.where(
        lax.broadcasted_iota(I32, (BD, BD), 0) < lax.broadcasted_iota(I32, (BD, BD), 1),
        F32(1),
        F32(0),
    ).astype(BF)
    before = jnp.dot(ohf.astype(BF), upper, preferred_element_type=F32)
    rank = jnp.sum(before * ohf, axis=0, keepdims=True).astype(I32)
    rw = row_v[...]
    here = beta == lax.broadcasted_iota(I32, (8, BD), 0)
    high = jnp.where(here, (rw // 64).astype(F32), F32(0)).astype(BF)
    low = jnp.where(here, (rw % 64).astype(F32), F32(0)).astype(BF)
    lane = plane * SLOTS + rank
    spot = jnp.where(
        lane == lax.broadcasted_iota(I32, (128, BD), 0), F32(1), F32(0)
    ).astype(BF)
    want = nt(high, spot) * 64.0 + nt(low, spot)
    req[...] = want.astype(I32).reshape(8, 1, 128)

    pl.semaphore_wait(bar, 22)
    for k in range(1, 8):
        send(req.at[k], t1.at[k], rq_s.at[0], rq_r.at[0], at(k // 2, k % 2, 0, 0))
    t1[0] = req[0]

    fetch[2].wait()
    uf = user_v[...].astype(F32)
    uu = (
        uf
        * lax.rsqrt(jnp.mean(uf * uf, axis=1, keepdims=True) + epsilon)
        / jnp.sqrt(F32(D))
    ).astype(BF)
    ug[0] = uu
    h = BD // 2
    top, bot = pl.ds(0, h), pl.ds(h, h)
    right, left, other = at(1, 0, 0, 0), at(3, 0, 0, 0), at(0, 1, 0, 0)

    def share(m, src, dst, to):
        send(src, dst, ag_s.at[m], ag_r.at[m], to)

    share(1, ug.at[0, top], ug.at[2, top], right)
    share(3, ug.at[0, bot], ug.at[4, bot], left)
    share(2, ug.at[0, bot], ug.at[2, bot], right)
    share(4, ug.at[0, top], ug.at[4, top], left)
    share(0, ug.at[0], ug.at[1], other)

    drain(t1.at[pl.ds(1, 7)], rq_r.at[0])
    for k in range(1, 16):
        send(t1, asked.at[k], rq_s.at[1], rq_r.at[1], at(0, 0, k % 4, k // 4))
    asked[0] = t1[...]

    place = pos * SLOTS + rank
    forth[...] = jnp.where(
        place == lax.broadcasted_iota(I32, (NDEV * SLOTS, BD), 0), F32(1), F32(0)
    ).astype(BF)
    diag = lax.broadcasted_iota(I32, (BD, BD), 0) == lax.broadcasted_iota(I32, (BD, BD), 1)
    down = jnp.sum(jnp.where(diag, place.astype(F32), F32(0)), axis=1, keepdims=True).astype(I32)
    back[...] = jnp.where(
        down == lax.broadcasted_iota(I32, (BD, NDEV * SLOTS), 1), F32(1), F32(0)
    ).astype(BF)
    rowq = lax.broadcasted_iota(I32, (NDEV * SLOTS, 128), 0)
    lanq = lax.broadcasted_iota(I32, (NDEV * SLOTS, 128), 1)
    grow = jnp.where(rowq // SLOTS == lanq, F32(1), F32(0)).astype(BF)
    ones = jnp.ones((128, 128), BF)
    fetch[4].wait()

    drain(asked.at[pl.ds(1, 15)], rq_r.at[1])
    parts = []
    for k in range(16):
        a = asked[k].reshape(8, 128)
        parts.append(pltpu.roll(a, (128 - 4 * k) % 128, 1) if k else a)
    flat = jnp.concatenate(parts, axis=0)
    hi = jnp.dot(grow, (flat // 64).astype(F32).astype(BF), preferred_element_type=F32)
    lo = jnp.dot(grow, (flat % 64).astype(F32).astype(BF), preferred_element_type=F32)
    mine = lanq == rowq % SLOTS
    picked = jnp.where(mine, hi * 64.0, F32(0)).astype(BF)
    picked2 = jnp.where(mine, lo, F32(0)).astype(BF)
    cols[...] = (
        jnp.dot(picked, ones, preferred_element_type=F32)
        + jnp.dot(picked2, ones, preferred_element_type=F32)
    ).astype(I32)

    for g in range(NCH):
        a = cols[g * CS : (g + 1) * CS, :]
        for j in range(ROWS // 128):
            hit = a == lax.broadcasted_iota(I32, (CS, 128), 1) + j * 128
            onehot[g * CS : (g + 1) * CS, j * 128 : (j + 1) * 128] = jnp.where(
                hit, F32(1), F32(0)
            ).astype(BF)
        found = jnp.dot(
            onehot[g * CS : (g + 1) * CS, :], table_v[...], preferred_element_type=F32
        )
        reply[g * CH : (g + 1) * CH] = found.astype(BF).reshape(CH, SLOTS, D)
        for i in range(max(1, g * CH), (g + 1) * CH):
            xi, ga, ze, et = split(i)
            to = at(4 - xi, ga, 4 - ze, 4 - et)
            send(reply.at[i], emb.at[i], rp_s, rp_r, to)
        if g == 0:
            drain(ug.at[2, top], ag_r.at[1])
            share(5, ug.at[2, top], ug.at[6, top], right)
            drain(ug.at[4, bot], ag_r.at[3])
            share(6, ug.at[4, bot], ug.at[6, bot], left)
        if g == 1:
            drain(ug.at[2, bot], ag_r.at[2])
            share(7, ug.at[2], ug.at[3], other)
            drain(ug.at[4, top], ag_r.at[4])
            share(8, ug.at[4], ug.at[5], other)
    emb[0] = reply[0]
    eye = lax.broadcasted_iota(I32, (128, 128), 0) == lax.broadcasted_iota(I32, (128, 128), 1)
    for g in range(NCH):
        a = cols[g * CS : (g + 1) * CS, :]
        askrow_out[:, g * CS : (g + 1) * CS] = jnp.broadcast_to(
            jnp.sum(jnp.where(eye, a, 0), axis=0, keepdims=True), (8, CS)
        )

    drain(ug.at[6, top], ag_r.at[5])
    share(9, ug.at[6, top], ug.at[7, top], other)
    drain(ug.at[6, bot], ag_r.at[6])
    share(10, ug.at[6, bot], ug.at[7, bot], other)
    drain(ug.at[1], ag_r.at[0])
    drain(ug.at[3], ag_r.at[7])
    drain(ug.at[5], ag_r.at[8])
    fetch[3].wait()

    drain(emb.at[pl.ds(1, NDEV - 1)], rp_r)
    e = jnp.dot(
        back[...], emb[...].reshape(NDEV * SLOTS, D), preferred_element_type=F32
    ).astype(BF)
    root = jnp.sqrt(F32(D))
    hid = jnp.dot(e, w_v[...], preferred_element_type=F32)
    rs = lax.rsqrt(jnp.mean(hid * hid, axis=1, keepdims=True) + epsilon)
    iv = (hid * rs / root).astype(BF)
    uf2 = ug[0].astype(F32)
    positive = jnp.sum(iv.astype(F32) * uf2, axis=1, keepdims=True) * score_scale
    drain(ug.at[7, top], ag_r.at[9])
    drain(ug.at[7, bot], ag_r.at[10])
    tot = jnp.zeros((BD, 1), F32)
    for k in range(8):
        ex = jnp.exp(nt(iv, ug[k]) * score_scale)
        tot = tot + jnp.sum(ex, axis=1, keepdims=True)
        exb[:, k * BD : (k + 1) * BD] = ex.astype(BF)
    mix = jnp.dot(exb[...], ug[...].reshape(8 * BD, D), preferred_element_type=F32)
    xent = jnp.log(tot) - positive
    cw = 1.0 / (1.0 + xent / cauchy_scale)
    dvec = cw * score_scale * (mix / tot - uf2)
    inner = jnp.sum(hid * dvec, axis=1, keepdims=True)
    dh = (rs / root * (dvec - hid * rs * rs * inner / D)).astype(BF)

    wgs[...] = tn(e, dh).astype(BF).reshape(8, 64, D)
    for k in range(4):
        send(wgs.at[k * 2 + 1 - c], wgr.at[k], wg_s.at[0], wg_r.at[0], other)

    drow = nt(dh, w_v[...]).astype(BF)
    for g in range(NCH):
        part = jnp.dot(forth[g * CS : (g + 1) * CS, :], drow, preferred_element_type=F32)
        drs[g * CH : (g + 1) * CH] = part.astype(BF).reshape(CH, SLOTS, D)
        for i in range(max(1, g * CH), (g + 1) * CH):
            send(drs.at[i], dr.at[i], gr_s, gr_r, at(*split(i)))
    dr[0] = drs[0]

    drain(wgr, wg_r.at[0])
    for k in range(4):
        both = wgs[k * 2 + c].astype(F32) + wgr[k].astype(F32)
        wg2[k * 16 : (k + 1) * 16] = both.astype(BF).reshape(16, 4, D)
    for j in range(1, 64):
        xi, ze, et = j // 16, (j // 4) % 4, j % 4
        src = wg2.at[xs[xi] * 8 + zs[ze] + ys[et]]
        send(src, wg3.at[j], wg_s.at[1], wg_r.at[1], at(xi, 0, ze, et))
    wg3[0] = wg2[x * 16 + z * 4 + y]

    drain(dr.at[pl.ds(1, NDEV - 1)], gr_r)
    drow_out[...] = dr[...].reshape(NDEV * SLOTS, D)
    drain(wg3.at[pl.ds(1, 63)], wg_r.at[1])
    wg_out[...] = jnp.sum(wg3[...].astype(F32), axis=0)

    drain(t1.at[pl.ds(1, 7)], rq_s.at[0])
    drain(asked.at[pl.ds(1, 15)], rq_s.at[1])
    drain(ug.at[0], ag_s.at[0])
    for m in (1, 2, 3, 4, 5, 6, 9, 10):
        drain(ug.at[0, top], ag_s.at[m])
    for m in (7, 8):
        drain(ug.at[0], ag_s.at[m])
    drain(reply.at[pl.ds(1, NDEV - 1)], rp_s)
    drain(drs.at[pl.ds(1, NDEV - 1)], gr_s)
    drain(wgr, wg_s.at[0])
    drain(wg2.at[pl.ds(1, 63)], wg_s.at[1])


def table_kernel(ask_ref, drow_ref, out_ref):
    n = out_ref.shape[0]
    base = pl.program_id(0) * n
    hit = ask_ref[0:1, :] == lax.broadcasted_iota(I32, (n, NDEV * SLOTS), 0) + base
    mat = jnp.where(hit, F32(1), F32(0)).astype(BF)
    out_ref[...] = jnp.dot(mat, drow_ref[...], preferred_element_type=F32).astype(BF)


def local(user_vectors, item_table, tower_weight, item_owner, item_row):
    dma = pltpu.SemaphoreType.DMA
    vm = pl.BlockSpec(memory_space=pltpu.VMEM)
    n = NDEV * SLOTS
    scratch = [
        pltpu.VMEM((BD, D), BF),
        pltpu.VMEM((D, D), BF),
        pltpu.VMEM((1, BD), I32),
        pltpu.VMEM((1, BD), I32),
        pltpu.VMEM((ROWS, D), BF),
        pltpu.VMEM((8, 1, 128), I32),
        pltpu.VMEM((8, 1, 128), I32),
        pltpu.VMEM((16, 8, 1, 128), I32),
        pltpu.VMEM((n, 128), I32),
        pltpu.VMEM((NDEV, SLOTS, D), BF),
        pltpu.VMEM((NDEV, SLOTS, D), BF),
        pltpu.VMEM((NDEV, SLOTS, D), BF),
        pltpu.VMEM((NDEV, SLOTS, D), BF),
        pltpu.VMEM((8, BD, D), BF),
        pltpu.VMEM((BD, n), BF),
        pltpu.VMEM((n, BD), BF),
        pltpu.VMEM((BD, 8 * BD), BF),
        pltpu.VMEM((n, ROWS), BF),
        pltpu.VMEM((8, 64, D), BF),
        pltpu.VMEM((4, 64, D), BF),
        pltpu.VMEM((64, 4, D), BF),
        pltpu.VMEM((64, 4, D), BF),
        dma((5,)),
        dma((11,)),
        dma((11,)),
        dma((2,)),
        dma((2,)),
        dma,
        dma,
        dma,
        dma,
        dma((2,)),
        dma((2,)),
    ]
    drow, ask, wgrad = pl.pallas_call(
        step_kernel,
        out_shape=(
            jax.ShapeDtypeStruct((n, D), BF),
            jax.ShapeDtypeStruct((8, n), I32),
            jax.ShapeDtypeStruct((4, D), F32),
        ),
        in_specs=[pl.BlockSpec(memory_space=pl.ANY)] * 5,
        out_specs=(vm, vm, vm),
        scratch_shapes=scratch,
        compiler_params=pltpu.CompilerParams(
            collective_id=0, has_side_effects=True, vmem_limit_bytes=60 * 1024 * 1024
        ),
    )(user_vectors, item_table, tower_weight, item_owner.reshape(1, BD), item_row.reshape(1, BD))
    blk = 512
    tgrad = pl.pallas_call(
        table_kernel,
        grid=(ROWS // blk,),
        out_shape=jax.ShapeDtypeStruct((ROWS, D), BF),
        in_specs=[
            pl.BlockSpec((8, n), lambda i: (0, 0)),
            pl.BlockSpec((n, D), lambda i: (0, 0)),
        ],
        out_specs=pl.BlockSpec((blk, D), lambda i: (i, 0)),
    )(ask, drow)
    return tgrad, wgrad


def solution(mesh):
    return jax.shard_map(
        local,
        mesh=mesh,
        in_specs=(
            P(("batch", "item"), None),
            P(("batch", "item"), None),
            P(),
            P(("batch", "item"), None),
            P(("batch", "item")),
        ),
        out_specs=(P(("batch", "item"), None), P(("batch", "item"), None)),
        check_vma=False,
    )
```

```python
import functools

import jax
import jax.numpy as jnp
from jax import lax
from jax.experimental import pallas as pl
from jax.experimental.pallas import tpu as pltpu
from jax.sharding import PartitionSpec as P

epsilon = 1e-06
score_scale = 60.0
cauchy_scale = 4.0

MESH = pl.DeviceIdType.MESH
BF = jnp.bfloat16
F32 = jnp.float32
I32 = jnp.int32
D = 512
BD = 256
ROWS = 4096
SLOTS = 4
NDEV = 128
NCH = 4
CH = NDEV // NCH
CS = CH * SLOTS


def nt(a, b):
    return lax.dot_general(a, b, (((1,), (1,)), ((), ())), preferred_element_type=F32)


def tn(a, b):
    return lax.dot_general(a, b, (((0,), (0,)), ((), ())), preferred_element_type=F32)


def hops(i):
    xi, ga, ze, et = (i % 8) // 2, i % 2, (i // 8) % 4, i // 32
    return sum(min(k, 4 - k) for k in (xi, ze, et)) + 0.5 * ga


def chunk(g):
    return sorted([i for i in range(max(1, g * CH), (g + 1) * CH)], key=lambda i: -hops(i))


ORDER = (2, 1, 3, 0)


def step_kernel(
    user_ref,
    table_ref,
    w_ref,
    owner_ref,
    row_ref,
    drow_out,
    askrow_out,
    wg_out,
    user_v,
    w_v,
    owner_v,
    row_v,
    table_v,
    req,
    t1,
    asked,
    cols,
    reply,
    emb,
    drs,
    dr,
    ug,
    back,
    forth,
    exb,
    onehot,
    wgs,
    wgr,
    wg2,
    wg3,
    drn,
    askv,
    out_s,
    in_s,
    ag_s,
    ag_r,
    rq_s,
    rq_r,
    rp_s,
    rp_r,
    gr_s,
    gr_r,
    wg_s,
    wg_r,
):
    b, it = lax.axis_index("batch"), lax.axis_index("item")
    x, c = b // 2, lax.rem(b, 2)
    z, y = it // 4, lax.rem(it, 4)
    xs = [lax.rem(x + k, 4) * 2 for k in range(4)]
    cs = [lax.rem(c + k, 2) for k in range(2)]
    zs = [lax.rem(z + k, 4) * 4 for k in range(4)]
    ys = [lax.rem(y + k, 4) for k in range(4)]

    def at(xi, ga, ze, et):
        return (xs[xi % 4] + cs[ga % 2], zs[ze % 4] + ys[et % 4])

    def split(i):
        return (i % 8) // 2, i % 2, (i // 8) % 4, i // 32

    def send(src, dst, ss, rs, to):
        pltpu.make_async_remote_copy(
            src_ref=src, dst_ref=dst, send_sem=ss, recv_sem=rs, device_id=to, device_id_type=MESH
        ).start()

    def drain(ref, sem):
        pltpu.make_async_copy(ref, ref, sem).wait()

    fetch = [
        pltpu.make_async_copy(src, dst, in_s.at[k])
        for k, (src, dst) in enumerate(
            [
                (owner_ref, owner_v),
                (row_ref, row_v),
                (user_ref, user_v),
                (w_ref, w_v),
                (table_ref, table_v),
            ]
        )
    ]
    for cp in fetch:
        cp.start()
    bar = pltpu.get_barrier_semaphore()
    for k in range(1, 8):
        pl.semaphore_signal(bar, inc=1, device_id=at(k // 2, k % 2, 0, 0), device_id_type=MESH)
    for k in range(1, 16):
        pl.semaphore_signal(bar, inc=1, device_id=at(0, 0, k % 4, k // 4), device_id_type=MESH)

    fetch[0].wait()
    fetch[1].wait()
    ow = owner_v[...]
    ox, oc = ow // 32, (ow // 16) % 2
    oz, oy = (ow // 4) % 4, ow % 4
    rx, rc = (ox - x + 4) % 4, (oc - c + 2) % 2
    rz, ry = (oz - z + 4) % 4, (oy - y + 4) % 4
    beta = rx * 2 + rc
    plane = ry * 4 + rz
    pos = plane * 8 + beta
    ohf = jnp.where(pos == lax.broadcasted_iota(I32, (NDEV, BD), 0), F32(1), F32(0))
    upper = jnp.where(
        lax.broadcasted_iota(I32, (BD, BD), 0) < lax.broadcasted_iota(I32, (BD, BD), 1),
        F32(1),
        F32(0),
    ).astype(BF)
    before = jnp.dot(ohf.astype(BF), upper, preferred_element_type=F32)
    rank = jnp.sum(before * ohf, axis=0, keepdims=True).astype(I32)
    rw = row_v[...]
    here = beta == lax.broadcasted_iota(I32, (8, BD), 0)
    high = jnp.where(here, (rw // 64).astype(F32), F32(0)).astype(BF)
    low = jnp.where(here, (rw % 64).astype(F32), F32(0)).astype(BF)
    lane = plane * SLOTS + rank
    spot = jnp.where(
        lane == lax.broadcasted_iota(I32, (128, BD), 0), F32(1), F32(0)
    ).astype(BF)
    want = nt(high, spot) * 64.0 + nt(low, spot)
    req[...] = want.astype(I32).reshape(8, 1, 128)

    fetch[2].wait()
    uf = user_v[...].astype(F32)
    uu = (
        uf
        * lax.rsqrt(jnp.mean(uf * uf, axis=1, keepdims=True) + epsilon)
        / jnp.sqrt(F32(D))
    ).astype(BF)
    ug[0] = uu
    pl.semaphore_wait(bar, 22)
    for k in range(1, 8):
        send(req.at[k], t1.at[k], rq_s.at[0], rq_r.at[0], at(k // 2, k % 2, 0, 0))
    t1[0] = req[0]

    h = BD // 2
    top, bot = pl.ds(0, h), pl.ds(h, h)
    right, left, other = at(1, 0, 0, 0), at(3, 0, 0, 0), at(0, 1, 0, 0)

    def share(m, src, dst, to):
        send(src, dst, ag_s.at[m], ag_r.at[m], to)

    share(1, ug.at[0, top], ug.at[2, top], right)
    share(3, ug.at[0, bot], ug.at[4, bot], left)
    share(2, ug.at[0, bot], ug.at[2, bot], right)
    share(4, ug.at[0, top], ug.at[4, top], left)
    share(0, ug.at[0], ug.at[1], other)

    drain(t1.at[pl.ds(1, 7)], rq_r.at[0])
    for k in sorted(range(1, 16), key=lambda k: -hops(k * 8)):
        send(t1, asked.at[k], rq_s.at[1], rq_r.at[1], at(0, 0, k % 4, k // 4))
    asked[0] = t1[...]

    place = pos * SLOTS + rank
    forth[...] = jnp.where(
        place == lax.broadcasted_iota(I32, (NDEV * SLOTS, BD), 0), F32(1), F32(0)
    ).astype(BF)
    diag = lax.broadcasted_iota(I32, (BD, BD), 0) == lax.broadcasted_iota(I32, (BD, BD), 1)
    down = jnp.sum(jnp.where(diag, place.astype(F32), F32(0)), axis=1, keepdims=True).astype(I32)
    back[...] = jnp.where(
        down == lax.broadcasted_iota(I32, (BD, NDEV * SLOTS), 1), F32(1), F32(0)
    ).astype(BF)
    rowq = lax.broadcasted_iota(I32, (NDEV * SLOTS, 128), 0)
    lanq = lax.broadcasted_iota(I32, (NDEV * SLOTS, 128), 1)
    grow = jnp.where(rowq // SLOTS == lanq, F32(1), F32(0)).astype(BF)
    ones = jnp.ones((128, 128), BF)
    fetch[4].wait()

    drain(ug.at[2, top], ag_r.at[1])
    share(5, ug.at[2, top], ug.at[6, top], right)
    drain(ug.at[4, bot], ag_r.at[3])
    share(6, ug.at[4, bot], ug.at[6, bot], left)
    drain(asked.at[pl.ds(1, 15)], rq_r.at[1])
    parts = []
    for k in range(16):
        a = asked[k].reshape(8, 128)
        parts.append(pltpu.roll(a, (128 - 4 * k) % 128, 1) if k else a)
    flat = jnp.concatenate(parts, axis=0)
    hi = jnp.dot(grow, (flat // 64).astype(F32).astype(BF), preferred_element_type=F32)
    lo = jnp.dot(grow, (flat % 64).astype(F32).astype(BF), preferred_element_type=F32)
    mine = lanq == rowq % SLOTS
    picked = jnp.where(mine, hi * 64.0, F32(0)).astype(BF)
    picked2 = jnp.where(mine, lo, F32(0)).astype(BF)
    cols[...] = (
        jnp.dot(picked, ones, preferred_element_type=F32)
        + jnp.dot(picked2, ones, preferred_element_type=F32)
    ).astype(I32)

    for n, g in enumerate(ORDER):
        a = cols[g * CS : (g + 1) * CS, :]
        for j in range(ROWS // 128):
            hit = a == lax.broadcasted_iota(I32, (CS, 128), 1) + j * 128
            onehot[g * CS : (g + 1) * CS, j * 128 : (j + 1) * 128] = jnp.where(
                hit, F32(1), F32(0)
            ).astype(BF)
        found = jnp.dot(
            onehot[g * CS : (g + 1) * CS, :], table_v[...], preferred_element_type=F32
        )
        reply[g * CH : (g + 1) * CH] = found.astype(BF).reshape(CH, SLOTS, D)
        for i in chunk(g):
            xi, ga, ze, et = split(i)
            to = at(4 - xi, ga, 4 - ze, 4 - et)
            send(reply.at[i], emb.at[i], rp_s, rp_r, to)
        if n == 0:
            drain(ug.at[2, bot], ag_r.at[2])
            share(7, ug.at[2], ug.at[3], other)
            drain(ug.at[4, top], ag_r.at[4])
            share(8, ug.at[4], ug.at[5], other)
        if n == 3:
            drain(ug.at[6, top], ag_r.at[5])
            share(9, ug.at[6, top], ug.at[7, top], other)
            drain(ug.at[6, bot], ag_r.at[6])
            share(10, ug.at[6, bot], ug.at[7, bot], other)
    emb[0] = reply[0]
    eye = lax.broadcasted_iota(I32, (128, 128), 0) == lax.broadcasted_iota(I32, (128, 128), 1)
    for g in range(NCH):
        a = cols[g * CS : (g + 1) * CS, :]
        askv[:, g * CS : (g + 1) * CS] = jnp.broadcast_to(
            jnp.sum(jnp.where(eye, a, 0), axis=0, keepdims=True), (8, CS)
        )

    outs = [pltpu.make_async_copy(askv, askrow_out, out_s.at[0])]
    outs[0].start()
    drain(ug.at[1], ag_r.at[0])
    drain(ug.at[3], ag_r.at[7])
    drain(ug.at[5], ag_r.at[8])
    fetch[3].wait()

    drain(emb.at[pl.ds(1, NDEV - 1)], rp_r)
    e = jnp.dot(
        back[...], emb[...].reshape(NDEV * SLOTS, D), preferred_element_type=F32
    ).astype(BF)
    root = jnp.sqrt(F32(D))
    hid = jnp.dot(e, w_v[...], preferred_element_type=F32)
    rs = lax.rsqrt(jnp.mean(hid * hid, axis=1, keepdims=True) + epsilon)
    iv = (hid * rs / root).astype(BF)
    uf2 = ug[0].astype(F32)
    positive = jnp.sum(iv.astype(F32) * uf2, axis=1, keepdims=True) * score_scale
    drain(ug.at[7, top], ag_r.at[9])
    drain(ug.at[7, bot], ag_r.at[10])
    tot = jnp.zeros((BD, 1), F32)
    for k in range(8):
        ex = jnp.exp(nt(iv, ug[k]) * score_scale)
        tot = tot + jnp.sum(ex, axis=1, keepdims=True)
        exb[:, k * BD : (k + 1) * BD] = ex.astype(BF)
    mix = jnp.dot(exb[...], ug[...].reshape(8 * BD, D), preferred_element_type=F32)
    xent = jnp.log(tot) - positive
    cw = 1.0 / (1.0 + xent / cauchy_scale)
    dvec = cw * score_scale * (mix / tot - uf2)
    inner = jnp.sum(hid * dvec, axis=1, keepdims=True)
    dh = (rs / root * (dvec - hid * rs * rs * inner / D)).astype(BF)

    wgs[...] = tn(e, dh).astype(BF).reshape(8, 64, D)
    for k in range(4):
        send(wgs.at[k * 2 + 1 - c], wgr.at[k], wg_s.at[0], wg_r.at[0], other)

    drow = nt(dh, w_v[...]).astype(BF)
    for g in ORDER:
        part = jnp.dot(forth[g * CS : (g + 1) * CS, :], drow, preferred_element_type=F32)
        drs[g * CH : (g + 1) * CH] = part.astype(BF).reshape(CH, SLOTS, D)
        for i in chunk(g):
            send(drs.at[i], dr.at[i], gr_s, gr_r, at(*split(i)))
    dr[0] = drs[0]

    drain(wgr, wg_r.at[0])
    for k in range(4):
        both = wgs[k * 2 + c].astype(F32) + wgr[k].astype(F32)
        wg2[k * 16 : (k + 1) * 16] = both.astype(BF).reshape(16, 4, D)
    for j in sorted(range(1, 64), key=lambda j: -hops(j // 16 * 2 + j // 4 % 4 * 8 + j % 4 * 32)):
        xi, ze, et = j // 16, (j // 4) % 4, j % 4
        src = wg2.at[xs[xi] * 8 + zs[ze] + ys[et]]
        send(src, wg3.at[j], wg_s.at[1], wg_r.at[1], at(xi, 0, ze, et))
    wg3[0] = wg2[x * 16 + z * 4 + y]

    drain(dr.at[pl.ds(1, NDEV - 1)], gr_r)
    drn[...] = dr[...].reshape(NDEV * SLOTS, D)
    outs.append(pltpu.make_async_copy(drn, drow_out, out_s.at[1]))
    outs[1].start()
    drain(wg3.at[pl.ds(1, 63)], wg_r.at[1])
    wg_out[...] = jnp.sum(wg3[...].astype(F32), axis=0)

    for cp in outs:
        cp.wait()
    drain(t1.at[pl.ds(1, 7)], rq_s.at[0])
    drain(asked.at[pl.ds(1, 15)], rq_s.at[1])
    drain(ug.at[0], ag_s.at[0])
    for m in (1, 2, 3, 4, 5, 6, 9, 10):
        drain(ug.at[0, top], ag_s.at[m])
    for m in (7, 8):
        drain(ug.at[0], ag_s.at[m])
    drain(reply.at[pl.ds(1, NDEV - 1)], rp_s)
    drain(drs.at[pl.ds(1, NDEV - 1)], gr_s)
    drain(wgr, wg_s.at[0])
    drain(wg2.at[pl.ds(1, 63)], wg_s.at[1])


CUTS = (0, 256, 512, 768, 1024, 1280, 1536, 1792, 2048, 2304, 2560, 2816, 3072, 3328, 3584, 3840, 4096)


def table_kernel(ask_ref, drow_ref, wg_ref, out_ref, wg_out, buf, sems):
    copies = []
    for k, (lo, hi) in enumerate(zip(CUTS[:-1], CUTS[1:])):
        hit = ask_ref[0:1, :] == lax.broadcasted_iota(I32, (hi - lo, NDEV * SLOTS), 0) + lo
        mat = jnp.where(hit, F32(1), F32(0)).astype(BF)
        buf[lo:hi, :] = jnp.dot(mat, drow_ref[...], preferred_element_type=F32).astype(BF)
        rows = pl.ds(lo, hi - lo)
        copies.append(pltpu.make_async_copy(buf.at[rows], out_ref.at[rows], sems.at[k]))
        copies[-1].start()
    wg_out[...] = wg_ref[...]
    for cp in copies:
        cp.wait()


def local(user_vectors, item_table, tower_weight, item_owner, item_row):
    dma = pltpu.SemaphoreType.DMA
    vm = pl.BlockSpec(memory_space=pltpu.VMEM)
    hbm = pl.BlockSpec(memory_space=pl.ANY)
    n = NDEV * SLOTS
    scratch = [
        pltpu.VMEM((BD, D), BF),
        pltpu.VMEM((D, D), BF),
        pltpu.VMEM((1, BD), I32),
        pltpu.VMEM((1, BD), I32),
        pltpu.VMEM((ROWS, D), BF),
        pltpu.VMEM((8, 1, 128), I32),
        pltpu.VMEM((8, 1, 128), I32),
        pltpu.VMEM((16, 8, 1, 128), I32),
        pltpu.VMEM((n, 128), I32),
        pltpu.VMEM((NDEV, SLOTS, D), BF),
        pltpu.VMEM((NDEV, SLOTS, D), BF),
        pltpu.VMEM((NDEV, SLOTS, D), BF),
        pltpu.VMEM((NDEV, SLOTS, D), BF),
        pltpu.VMEM((8, BD, D), BF),
        pltpu.VMEM((BD, n), BF),
        pltpu.VMEM((n, BD), BF),
        pltpu.VMEM((BD, 8 * BD), BF),
        pltpu.VMEM((n, ROWS), BF),
        pltpu.VMEM((8, 64, D), BF),
        pltpu.VMEM((4, 64, D), BF),
        pltpu.VMEM((64, 4, D), BF),
        pltpu.VMEM((64, 4, D), BF),
        pltpu.VMEM((n, D), BF),
        pltpu.VMEM((8, n), I32),
        dma((2,)),
        dma((5,)),
        dma((11,)),
        dma((11,)),
        dma((2,)),
        dma((2,)),
        dma,
        dma,
        dma,
        dma,
        dma((2,)),
        dma((2,)),
    ]
    drow, ask, wgrad = pl.pallas_call(
        step_kernel,
        out_shape=(
            jax.ShapeDtypeStruct((n, D), BF),
            jax.ShapeDtypeStruct((8, n), I32),
            jax.ShapeDtypeStruct((4, D), F32),
        ),
        in_specs=[pl.BlockSpec(memory_space=pl.ANY)] * 5,
        out_specs=(hbm, hbm, vm),
        scratch_shapes=scratch,
        compiler_params=pltpu.CompilerParams(
            collective_id=0, has_side_effects=True, vmem_limit_bytes=60 * 1024 * 1024
        ),
    )(user_vectors, item_table, tower_weight, item_owner.reshape(1, BD), item_row.reshape(1, BD))
    return pl.pallas_call(
        table_kernel,
        out_shape=(
            jax.ShapeDtypeStruct((ROWS, D), BF),
            jax.ShapeDtypeStruct((4, D), F32),
        ),
        in_specs=[vm, vm, vm],
        out_specs=(hbm, vm),
        scratch_shapes=[pltpu.VMEM((ROWS, D), BF), dma((len(CUTS) - 1,))],
    )(ask, drow, wgrad)


def solution(mesh):
    return jax.shard_map(
        local,
        mesh=mesh,
        in_specs=(
            P(("batch", "item"), None),
            P(("batch", "item"), None),
            P(),
            P(("batch", "item"), None),
            P(("batch", "item")),
        ),
        out_specs=(P(("batch", "item"), None), P(("batch", "item"), None)),
        check_vma=False,
    )
```

```python
import functools

import jax
import jax.numpy as jnp
from jax import lax
from jax.experimental import pallas as pl
from jax.experimental.pallas import tpu as pltpu
from jax.sharding import PartitionSpec as P

epsilon = 1e-06
score_scale = 60.0
cauchy_scale = 4.0

MESH = pl.DeviceIdType.MESH
BF = jnp.bfloat16
F32 = jnp.float32
I32 = jnp.int32
D = 512
BD = 256
ROWS = 4096
SLOTS = 4
NDEV = 128
NCH = 4
CH = NDEV // NCH
CS = CH * SLOTS


def nt(a, b):
    return lax.dot_general(a, b, (((1,), (1,)), ((), ())), preferred_element_type=F32)


def tn(a, b):
    return lax.dot_general(a, b, (((0,), (0,)), ((), ())), preferred_element_type=F32)


def hops(i):
    xi, ga, ze, et = (i % 8) // 2, i % 2, (i // 8) % 4, i // 32
    return sum(min(k, 4 - k) for k in (xi, ze, et)) + 0.5 * ga


def chunk(g):
    return sorted([i for i in range(max(1, g * CH), (g + 1) * CH)], key=lambda i: -hops(i))


ORDER = (2, 1, 3, 0)


def step_kernel(
    user_ref,
    table_ref,
    w_ref,
    owner_ref,
    row_ref,
    drow_out,
    askrow_out,
    wg_out,
    user_v,
    w_v,
    owner_v,
    row_v,
    table_v,
    req,
    t1,
    asked,
    cols,
    reply,
    emb,
    drs,
    ug,
    back,
    forth,
    exb,
    onehot,
    wgs,
    wgr,
    wg2,
    askv,
    out_s,
    in_s,
    ag_s,
    ag_r,
    rq_s,
    rq_r,
    rp_s,
    rp_r,
    gr_s,
    gr_r,
    wg_s,
    wg_r,
):
    b, it = lax.axis_index("batch"), lax.axis_index("item")
    x, c = b // 2, lax.rem(b, 2)
    z, y = it // 4, lax.rem(it, 4)
    xs = [lax.rem(x + k, 4) * 2 for k in range(4)]
    cs = [lax.rem(c + k, 2) for k in range(2)]
    zs = [lax.rem(z + k, 4) * 4 for k in range(4)]
    ys = [lax.rem(y + k, 4) for k in range(4)]

    def at(xi, ga, ze, et):
        return (xs[xi % 4] + cs[ga % 2], zs[ze % 4] + ys[et % 4])

    def split(i):
        return (i % 8) // 2, i % 2, (i // 8) % 4, i // 32

    def send(src, dst, ss, rs, to):
        pltpu.make_async_remote_copy(
            src_ref=src, dst_ref=dst, send_sem=ss, recv_sem=rs, device_id=to, device_id_type=MESH
        ).start()

    def drain(ref, sem):
        pltpu.make_async_copy(ref, ref, sem).wait()

    fetch = [
        pltpu.make_async_copy(src, dst, in_s.at[k])
        for k, (src, dst) in enumerate(
            [
                (owner_ref, owner_v),
                (row_ref, row_v),
                (user_ref, user_v),
                (w_ref, w_v),
                (table_ref, table_v),
            ]
        )
    ]
    for cp in fetch:
        cp.start()
    bar = pltpu.get_barrier_semaphore()
    for k in range(1, 8):
        pl.semaphore_signal(bar, inc=1, device_id=at(k // 2, k % 2, 0, 0), device_id_type=MESH)
    for k in range(1, 16):
        pl.semaphore_signal(bar, inc=1, device_id=at(0, 0, k % 4, k // 4), device_id_type=MESH)

    fetch[0].wait()
    fetch[1].wait()
    ow = owner_v[...]
    ox, oc = ow // 32, (ow // 16) % 2
    oz, oy = (ow // 4) % 4, ow % 4
    rx, rc = (ox - x + 4) % 4, (oc - c + 2) % 2
    rz, ry = (oz - z + 4) % 4, (oy - y + 4) % 4
    beta = rx * 2 + rc
    plane = ry * 4 + rz
    pos = plane * 8 + beta
    ohf = jnp.where(pos == lax.broadcasted_iota(I32, (NDEV, BD), 0), F32(1), F32(0))
    upper = jnp.where(
        lax.broadcasted_iota(I32, (BD, BD), 0) < lax.broadcasted_iota(I32, (BD, BD), 1),
        F32(1),
        F32(0),
    ).astype(BF)
    before = jnp.dot(ohf.astype(BF), upper, preferred_element_type=F32)
    rank = jnp.sum(before * ohf, axis=0, keepdims=True).astype(I32)
    rw = row_v[...]
    here = beta == lax.broadcasted_iota(I32, (8, BD), 0)
    high = jnp.where(here, (rw // 64).astype(F32), F32(0)).astype(BF)
    low = jnp.where(here, (rw % 64).astype(F32), F32(0)).astype(BF)
    lane = plane * SLOTS + rank
    spot = jnp.where(
        lane == lax.broadcasted_iota(I32, (128, BD), 0), F32(1), F32(0)
    ).astype(BF)
    want = nt(high, spot) * 64.0 + nt(low, spot)
    req[...] = want.astype(I32).reshape(8, 1, 128)

    fetch[2].wait()
    uf = user_v[...].astype(F32)
    uu = (
        uf
        * lax.rsqrt(jnp.mean(uf * uf, axis=1, keepdims=True) + epsilon)
        / jnp.sqrt(F32(D))
    ).astype(BF)
    ug[0] = uu
    pl.semaphore_wait(bar, 22)
    for k in range(1, 8):
        send(req.at[k], t1.at[k], rq_s.at[0], rq_r.at[0], at(k // 2, k % 2, 0, 0))
    t1[0] = req[0]

    h = BD // 2
    top, bot = pl.ds(0, h), pl.ds(h, h)
    right, left, other = at(1, 0, 0, 0), at(3, 0, 0, 0), at(0, 1, 0, 0)

    def share(m, src, dst, to):
        send(src, dst, ag_s.at[m], ag_r.at[m], to)

    share(1, ug.at[0, top], ug.at[2, top], right)
    share(3, ug.at[0, bot], ug.at[4, bot], left)
    share(2, ug.at[0, bot], ug.at[2, bot], right)
    share(4, ug.at[0, top], ug.at[4, top], left)
    share(0, ug.at[0], ug.at[1], other)

    drain(t1.at[pl.ds(1, 7)], rq_r.at[0])
    for k in sorted(range(1, 16), key=lambda k: -hops(k * 8)):
        send(t1, asked.at[k], rq_s.at[1], rq_r.at[1], at(0, 0, k % 4, k // 4))
    asked[0] = t1[...]

    place = pos * SLOTS + rank
    forth[...] = jnp.where(
        place == lax.broadcasted_iota(I32, (NDEV * SLOTS, BD), 0), F32(1), F32(0)
    ).astype(BF)
    diag = lax.broadcasted_iota(I32, (BD, BD), 0) == lax.broadcasted_iota(I32, (BD, BD), 1)
    down = jnp.sum(jnp.where(diag, place.astype(F32), F32(0)), axis=1, keepdims=True).astype(I32)
    back[...] = jnp.where(
        down == lax.broadcasted_iota(I32, (BD, NDEV * SLOTS), 1), F32(1), F32(0)
    ).astype(BF)
    rowq = lax.broadcasted_iota(I32, (NDEV * SLOTS, 128), 0)
    lanq = lax.broadcasted_iota(I32, (NDEV * SLOTS, 128), 1)
    grow = jnp.where(rowq // SLOTS == lanq, F32(1), F32(0)).astype(BF)
    ones = jnp.ones((128, 128), BF)
    fetch[4].wait()

    drain(ug.at[2, top], ag_r.at[1])
    share(5, ug.at[2, top], ug.at[6, top], right)
    drain(ug.at[4, bot], ag_r.at[3])
    share(6, ug.at[4, bot], ug.at[6, bot], left)
    drain(asked.at[pl.ds(1, 15)], rq_r.at[1])
    parts = []
    for k in range(16):
        a = asked[k].reshape(8, 128)
        parts.append(pltpu.roll(a, (128 - 4 * k) % 128, 1) if k else a)
    flat = jnp.concatenate(parts, axis=0)
    hi = jnp.dot(grow, (flat // 64).astype(F32).astype(BF), preferred_element_type=F32)
    lo = jnp.dot(grow, (flat % 64).astype(F32).astype(BF), preferred_element_type=F32)
    mine = lanq == rowq % SLOTS
    picked = jnp.where(mine, hi * 64.0, F32(0)).astype(BF)
    picked2 = jnp.where(mine, lo, F32(0)).astype(BF)
    cols[...] = (
        jnp.dot(picked, ones, preferred_element_type=F32)
        + jnp.dot(picked2, ones, preferred_element_type=F32)
    ).astype(I32)

    for n, g in enumerate(ORDER):
        a = cols[g * CS : (g + 1) * CS, :]
        for j in range(ROWS // 128):
            hit = a == lax.broadcasted_iota(I32, (CS, 128), 1) + j * 128
            onehot[g * CS : (g + 1) * CS, j * 128 : (j + 1) * 128] = jnp.where(
                hit, F32(1), F32(0)
            ).astype(BF)
        found = jnp.dot(
            onehot[g * CS : (g + 1) * CS, :], table_v[...], preferred_element_type=F32
        )
        reply[g * CH : (g + 1) * CH] = found.astype(BF).reshape(CH, SLOTS, D)
        for i in chunk(g):
            xi, ga, ze, et = split(i)
            to = at(4 - xi, ga, 4 - ze, 4 - et)
            send(reply.at[i], emb.at[i], rp_s, rp_r, to)
        if n == 0:
            drain(ug.at[2, bot], ag_r.at[2])
            share(7, ug.at[2], ug.at[3], other)
            drain(ug.at[4, top], ag_r.at[4])
            share(8, ug.at[4], ug.at[5], other)
        if n == 3:
            drain(ug.at[6, top], ag_r.at[5])
            share(9, ug.at[6, top], ug.at[7, top], other)
            drain(ug.at[6, bot], ag_r.at[6])
            share(10, ug.at[6, bot], ug.at[7, bot], other)
    emb[0] = reply[0]
    eye = lax.broadcasted_iota(I32, (128, 128), 0) == lax.broadcasted_iota(I32, (128, 128), 1)
    for g in range(NCH):
        a = cols[g * CS : (g + 1) * CS, :]
        askv[:, g * CS : (g + 1) * CS] = jnp.broadcast_to(
            jnp.sum(jnp.where(eye, a, 0), axis=0, keepdims=True), (8, CS)
        )

    outs = [pltpu.make_async_copy(askv, askrow_out, out_s.at[0])]
    outs[0].start()
    drain(ug.at[1], ag_r.at[0])
    drain(ug.at[3], ag_r.at[7])
    drain(ug.at[5], ag_r.at[8])
    fetch[3].wait()

    drain(emb.at[pl.ds(1, NDEV - 1)], rp_r)
    e = jnp.dot(
        back[...], emb[...].reshape(NDEV * SLOTS, D), preferred_element_type=F32
    ).astype(BF)
    root = jnp.sqrt(F32(D))
    hid = jnp.dot(e, w_v[...], preferred_element_type=F32)
    rs = lax.rsqrt(jnp.mean(hid * hid, axis=1, keepdims=True) + epsilon)
    iv = (hid * rs / root).astype(BF)
    uf2 = ug[0].astype(F32)
    positive = jnp.sum(iv.astype(F32) * uf2, axis=1, keepdims=True) * score_scale
    drain(ug.at[7, top], ag_r.at[9])
    drain(ug.at[7, bot], ag_r.at[10])
    tot = jnp.zeros((BD, 1), F32)
    for k in range(8):
        ex = jnp.exp(nt(iv, ug[k]) * score_scale)
        tot = tot + jnp.sum(ex, axis=1, keepdims=True)
        exb[:, k * BD : (k + 1) * BD] = ex.astype(BF)
    mix = jnp.dot(exb[...], ug[...].reshape(8 * BD, D), preferred_element_type=F32)
    xent = jnp.log(tot) - positive
    cw = 1.0 / (1.0 + xent / cauchy_scale)
    dvec = cw * score_scale * (mix / tot - uf2)
    inner = jnp.sum(hid * dvec, axis=1, keepdims=True)
    dh = (rs / root * (dvec - hid * rs * rs * inner / D)).astype(BF)

    wgs[...] = tn(e, dh).astype(BF).reshape(8, 64, D)
    for k in range(4):
        send(wgs.at[k * 2 + 1 - c], wgr.at[k], wg_s.at[0], wg_r.at[0], other)

    drow = nt(dh, w_v[...]).astype(BF)
    for g in ORDER:
        part = jnp.dot(forth[g * CS : (g + 1) * CS, :], drow, preferred_element_type=F32)
        drs[g * CH : (g + 1) * CH] = part.astype(BF).reshape(CH, SLOTS, D)
        for i in chunk(g):
            send(drs.at[i], drow_out.at[i], gr_s, gr_r, at(*split(i)))
    outs.append(pltpu.make_async_copy(drs.at[0], drow_out.at[0], out_s.at[1]))
    outs[1].start()

    drain(wgr, wg_r.at[0])
    for k in range(4):
        both = wgs[k * 2 + c].astype(F32) + wgr[k].astype(F32)
        wg2[k * 16 : (k + 1) * 16] = both.astype(BF).reshape(16, 4, D)
    for j in sorted(range(1, 64), key=lambda j: -hops(j // 16 * 2 + j // 4 % 4 * 8 + j % 4 * 32)):
        xi, ze, et = j // 16, (j // 4) % 4, j % 4
        src = wg2.at[xs[xi] * 8 + zs[ze] + ys[et]]
        send(src, wg_out.at[j], wg_s.at[1], wg_r.at[1], at(xi, 0, ze, et))
    outs.append(
        pltpu.make_async_copy(wg2.at[x * 16 + z * 4 + y], wg_out.at[0], out_s.at[2])
    )
    outs[2].start()

    drain(drow_out.at[pl.ds(1, NDEV - 1)], gr_r)
    drain(wg_out.at[pl.ds(1, 63)], wg_r.at[1])

    for cp in outs:
        cp.wait()
    drain(t1.at[pl.ds(1, 7)], rq_s.at[0])
    drain(asked.at[pl.ds(1, 15)], rq_s.at[1])
    drain(ug.at[0], ag_s.at[0])
    for m in (1, 2, 3, 4, 5, 6, 9, 10):
        drain(ug.at[0, top], ag_s.at[m])
    for m in (7, 8):
        drain(ug.at[0], ag_s.at[m])
    drain(reply.at[pl.ds(1, NDEV - 1)], rp_s)
    drain(drs.at[pl.ds(1, NDEV - 1)], gr_s)
    drain(wgr, wg_s.at[0])
    drain(wg2.at[pl.ds(1, 63)], wg_s.at[1])


CUTS = (0, 256, 512, 768, 1024, 1280, 1536, 1792, 2048, 2304, 2560, 2816, 3072, 3328, 3584, 3840, 4096)


def table_kernel(ask_ref, drow_ref, wg_ref, out_ref, wg_out, rows_v, wg_v, buf, sems):
    bring = pltpu.make_async_copy(wg_ref, wg_v, sems.at[0])
    bring.start()
    rows_v[...] = drow_ref[...].reshape(NDEV * SLOTS, D)
    copies = []
    for k, (lo, hi) in enumerate(zip(CUTS[:-1], CUTS[1:])):
        hit = ask_ref[0:1, :] == lax.broadcasted_iota(I32, (hi - lo, NDEV * SLOTS), 0) + lo
        mat = jnp.where(hit, F32(1), F32(0)).astype(BF)
        buf[lo:hi, :] = jnp.dot(mat, rows_v[...], preferred_element_type=F32).astype(BF)
        rows = pl.ds(lo, hi - lo)
        copies.append(pltpu.make_async_copy(buf.at[rows], out_ref.at[rows], sems.at[k + 1]))
        copies[-1].start()
        if k == 8:
            bring.wait()
            wg_out[...] = jnp.sum(wg_v[...].astype(F32), axis=0)
    for cp in copies:
        cp.wait()


def local(user_vectors, item_table, tower_weight, item_owner, item_row):
    dma = pltpu.SemaphoreType.DMA
    vm = pl.BlockSpec(memory_space=pltpu.VMEM)
    hbm = pl.BlockSpec(memory_space=pl.ANY)
    n = NDEV * SLOTS
    scratch = [
        pltpu.VMEM((BD, D), BF),
        pltpu.VMEM((D, D), BF),
        pltpu.VMEM((1, BD), I32),
        pltpu.VMEM((1, BD), I32),
        pltpu.VMEM((ROWS, D), BF),
        pltpu.VMEM((8, 1, 128), I32),
        pltpu.VMEM((8, 1, 128), I32),
        pltpu.VMEM((16, 8, 1, 128), I32),
        pltpu.VMEM((n, 128), I32),
        pltpu.VMEM((NDEV, SLOTS, D), BF),
        pltpu.VMEM((NDEV, SLOTS, D), BF),
        pltpu.VMEM((NDEV, SLOTS, D), BF),
        pltpu.VMEM((8, BD, D), BF),
        pltpu.VMEM((BD, n), BF),
        pltpu.VMEM((n, BD), BF),
        pltpu.VMEM((BD, 8 * BD), BF),
        pltpu.VMEM((n, ROWS), BF),
        pltpu.VMEM((8, 64, D), BF),
        pltpu.VMEM((4, 64, D), BF),
        pltpu.VMEM((64, 4, D), BF),
        pltpu.VMEM((8, n), I32),
        dma((3,)),
        dma((5,)),
        dma((11,)),
        dma((11,)),
        dma((2,)),
        dma((2,)),
        dma,
        dma,
        dma,
        dma,
        dma((2,)),
        dma((2,)),
    ]
    drow, ask, shares = pl.pallas_call(
        step_kernel,
        out_shape=(
            jax.ShapeDtypeStruct((NDEV, SLOTS, D), BF),
            jax.ShapeDtypeStruct((8, n), I32),
            jax.ShapeDtypeStruct((64, 4, D), BF),
        ),
        in_specs=[pl.BlockSpec(memory_space=pl.ANY)] * 5,
        out_specs=(hbm, hbm, hbm),
        scratch_shapes=scratch,
        compiler_params=pltpu.CompilerParams(
            collective_id=0, has_side_effects=True, vmem_limit_bytes=60 * 1024 * 1024
        ),
    )(user_vectors, item_table, tower_weight, item_owner.reshape(1, BD), item_row.reshape(1, BD))
    return pl.pallas_call(
        table_kernel,
        out_shape=(
            jax.ShapeDtypeStruct((ROWS, D), BF),
            jax.ShapeDtypeStruct((4, D), F32),
        ),
        in_specs=[vm, vm, hbm],
        out_specs=(hbm, vm),
        scratch_shapes=[
            pltpu.VMEM((n, D), BF),
            pltpu.VMEM((64, 4, D), BF),
            pltpu.VMEM((ROWS, D), BF),
            dma((len(CUTS),)),
        ],
    )(ask, drow, shares)


def solution(mesh):
    return jax.shard_map(
        local,
        mesh=mesh,
        in_specs=(
            P(("batch", "item"), None),
            P(("batch", "item"), None),
            P(),
            P(("batch", "item"), None),
            P(("batch", "item")),
        ),
        out_specs=(P(("batch", "item"), None), P(("batch", "item"), None)),
        check_vma=False,
    )
```

```python
import functools

import jax
import jax.numpy as jnp
from jax import lax
from jax.experimental import pallas as pl
from jax.experimental.pallas import tpu as pltpu
from jax.sharding import PartitionSpec as P

epsilon = 1e-06
score_scale = 60.0
cauchy_scale = 4.0

MESH = pl.DeviceIdType.MESH
BF = jnp.bfloat16
F32 = jnp.float32
I32 = jnp.int32
D = 512
BD = 256
ROWS = 4096
SLOTS = 4
NDEV = 128
NCH = 4
CH = NDEV // NCH
CS = CH * SLOTS


def nt(a, b):
    return lax.dot_general(a, b, (((1,), (1,)), ((), ())), preferred_element_type=F32)


def tn(a, b):
    return lax.dot_general(a, b, (((0,), (0,)), ((), ())), preferred_element_type=F32)


def hops(i):
    xi, ga, ze, et = (i % 8) // 2, i % 2, (i // 8) % 4, i // 32
    return sum(min(k, 4 - k) for k in (xi, ze, et)) + 0.5 * ga


def chunk(g):
    return sorted([i for i in range(max(1, g * CH), (g + 1) * CH)], key=lambda i: -hops(i))


ORDER = (2, 1, 3, 0)


def step_kernel(
    user_ref,
    table_ref,
    w_ref,
    owner_ref,
    row_ref,
    drow_out,
    askrow_out,
    wg_out,
    user_v,
    w_v,
    owner_v,
    row_v,
    table_v,
    req,
    t1,
    asked,
    cols,
    reply,
    emb,
    drs,
    ug,
    back,
    forth,
    exb,
    onehot,
    wgs,
    wgr,
    wg2,
    askv,
    out_s,
    in_s,
    ag_s,
    ag_r,
    rq_s,
    rq_r,
    rp_s,
    rp_r,
    gr_s,
    gr_r,
    wg_s,
    wg_r,
):
    b, it = lax.axis_index("batch"), lax.axis_index("item")
    x, c = b // 2, lax.rem(b, 2)
    z, y = it // 4, lax.rem(it, 4)
    xs = [lax.rem(x + k, 4) * 2 for k in range(4)]
    cs = [lax.rem(c + k, 2) for k in range(2)]
    zs = [lax.rem(z + k, 4) * 4 for k in range(4)]
    ys = [lax.rem(y + k, 4) for k in range(4)]

    def at(xi, ga, ze, et):
        return (xs[xi % 4] + cs[ga % 2], zs[ze % 4] + ys[et % 4])

    def split(i):
        return (i % 8) // 2, i % 2, (i // 8) % 4, i // 32

    def send(src, dst, ss, rs, to):
        pltpu.make_async_remote_copy(
            src_ref=src, dst_ref=dst, send_sem=ss, recv_sem=rs, device_id=to, device_id_type=MESH
        ).start()

    def drain(ref, sem):
        pltpu.make_async_copy(ref, ref, sem).wait()

    fetch = [
        pltpu.make_async_copy(src, dst, in_s.at[k])
        for k, (src, dst) in enumerate(
            [
                (owner_ref, owner_v),
                (row_ref, row_v),
                (user_ref, user_v),
                (w_ref, w_v),
                (table_ref, table_v),
            ]
        )
    ]
    for cp in fetch[:2]:
        cp.start()
    bar = pltpu.get_barrier_semaphore()
    for k in range(1, 8):
        pl.semaphore_signal(bar, inc=1, device_id=at(k // 2, k % 2, 0, 0), device_id_type=MESH)
    for k in range(1, 16):
        pl.semaphore_signal(bar, inc=1, device_id=at(0, 0, k % 4, k // 4), device_id_type=MESH)

    for cp in fetch[2:]:
        cp.start()

    fetch[0].wait()
    fetch[1].wait()
    ow = owner_v[...]
    ox, oc = ow // 32, (ow // 16) % 2
    oz, oy = (ow // 4) % 4, ow % 4
    rx, rc = (ox - x + 4) % 4, (oc - c + 2) % 2
    rz, ry = (oz - z + 4) % 4, (oy - y + 4) % 4
    beta = rx * 2 + rc
    plane = ry * 4 + rz
    pos = plane * 8 + beta
    ohf = jnp.where(pos == lax.broadcasted_iota(I32, (NDEV, BD), 0), F32(1), F32(0))
    upper = jnp.where(
        lax.broadcasted_iota(I32, (BD, BD), 0) < lax.broadcasted_iota(I32, (BD, BD), 1),
        F32(1),
        F32(0),
    ).astype(BF)
    before = jnp.dot(ohf.astype(BF), upper, preferred_element_type=F32)
    rank = jnp.sum(before * ohf, axis=0, keepdims=True).astype(I32)
    rw = row_v[...]
    here = beta == lax.broadcasted_iota(I32, (8, BD), 0)
    high = jnp.where(here, (rw // 64).astype(F32), F32(0)).astype(BF)
    low = jnp.where(here, (rw % 64).astype(F32), F32(0)).astype(BF)
    lane = plane * SLOTS + rank
    spot = jnp.where(
        lane == lax.broadcasted_iota(I32, (128, BD), 0), F32(1), F32(0)
    ).astype(BF)
    want = nt(high, spot) * 64.0 + nt(low, spot)
    req[...] = want.astype(I32).reshape(8, 1, 128)

    pl.semaphore_wait(bar, 22)
    for k in range(1, 8):
        send(req.at[k], t1.at[k], rq_s.at[0], rq_r.at[0], at(k // 2, k % 2, 0, 0))
    t1[0] = req[0]

    fetch[2].wait()
    uf = user_v[...].astype(F32)
    uu = (
        uf
        * lax.rsqrt(jnp.mean(uf * uf, axis=1, keepdims=True) + epsilon)
        / jnp.sqrt(F32(D))
    ).astype(BF)
    ug[0] = uu
    h = BD // 2
    top, bot = pl.ds(0, h), pl.ds(h, h)
    right, left, other = at(1, 0, 0, 0), at(3, 0, 0, 0), at(0, 1, 0, 0)

    def share(m, src, dst, to):
        send(src, dst, ag_s.at[m], ag_r.at[m], to)

    share(1, ug.at[0, top], ug.at[2, top], right)
    share(3, ug.at[0, bot], ug.at[4, bot], left)
    share(2, ug.at[0, bot], ug.at[2, bot], right)
    share(4, ug.at[0, top], ug.at[4, top], left)
    share(0, ug.at[0], ug.at[1], other)

    drain(t1.at[pl.ds(1, 7)], rq_r.at[0])
    for k in sorted(range(1, 16), key=lambda k: -hops(k * 8)):
        send(t1, asked.at[k], rq_s.at[1], rq_r.at[1], at(0, 0, k % 4, k // 4))
    asked[0] = t1[...]

    place = pos * SLOTS + rank
    forth[...] = jnp.where(
        place == lax.broadcasted_iota(I32, (NDEV * SLOTS, BD), 0), F32(1), F32(0)
    ).astype(BF)
    diag = lax.broadcasted_iota(I32, (BD, BD), 0) == lax.broadcasted_iota(I32, (BD, BD), 1)
    down = jnp.sum(jnp.where(diag, place.astype(F32), F32(0)), axis=1, keepdims=True).astype(I32)
    back[...] = jnp.where(
        down == lax.broadcasted_iota(I32, (BD, NDEV * SLOTS), 1), F32(1), F32(0)
    ).astype(BF)
    rowq = lax.broadcasted_iota(I32, (NDEV * SLOTS, 128), 0)
    lanq = lax.broadcasted_iota(I32, (NDEV * SLOTS, 128), 1)
    grow = jnp.where(rowq // SLOTS == lanq, F32(1), F32(0)).astype(BF)
    ones = jnp.ones((128, 128), BF)
    fetch[4].wait()

    drain(ug.at[2, top], ag_r.at[1])
    share(5, ug.at[2, top], ug.at[6, top], right)
    drain(ug.at[4, bot], ag_r.at[3])
    share(6, ug.at[4, bot], ug.at[6, bot], left)
    drain(asked.at[pl.ds(1, 15)], rq_r.at[1])
    parts = []
    for k in range(16):
        a = asked[k].reshape(8, 128)
        parts.append(pltpu.roll(a, (128 - 4 * k) % 128, 1) if k else a)
    flat = jnp.concatenate(parts, axis=0)
    hi = jnp.dot(grow, (flat // 64).astype(F32).astype(BF), preferred_element_type=F32)
    lo = jnp.dot(grow, (flat % 64).astype(F32).astype(BF), preferred_element_type=F32)
    mine = lanq == rowq % SLOTS
    picked = jnp.where(mine, hi * 64.0, F32(0)).astype(BF)
    picked2 = jnp.where(mine, lo, F32(0)).astype(BF)
    cols[...] = (
        jnp.dot(picked, ones, preferred_element_type=F32)
        + jnp.dot(picked2, ones, preferred_element_type=F32)
    ).astype(I32)

    for n, g in enumerate(ORDER):
        a = cols[g * CS : (g + 1) * CS, :]
        for j in range(ROWS // 128):
            hit = a == lax.broadcasted_iota(I32, (CS, 128), 1) + j * 128
            onehot[g * CS : (g + 1) * CS, j * 128 : (j + 1) * 128] = jnp.where(
                hit, F32(1), F32(0)
            ).astype(BF)
        found = jnp.dot(
            onehot[g * CS : (g + 1) * CS, :], table_v[...], preferred_element_type=F32
        )
        reply[g * CH : (g + 1) * CH] = found.astype(BF).reshape(CH, SLOTS, D)
        for i in chunk(g):
            xi, ga, ze, et = split(i)
            to = at(4 - xi, ga, 4 - ze, 4 - et)
            send(reply.at[i], emb.at[i], rp_s, rp_r, to)
        if n == 0:
            drain(ug.at[2, bot], ag_r.at[2])
            share(7, ug.at[2], ug.at[3], other)
            drain(ug.at[4, top], ag_r.at[4])
            share(8, ug.at[4], ug.at[5], other)
        if n == 3:
            drain(ug.at[6, top], ag_r.at[5])
            share(9, ug.at[6, top], ug.at[7, top], other)
            drain(ug.at[6, bot], ag_r.at[6])
            share(10, ug.at[6, bot], ug.at[7, bot], other)
    emb[0] = reply[0]
    eye = lax.broadcasted_iota(I32, (128, 128), 0) == lax.broadcasted_iota(I32, (128, 128), 1)
    for g in range(NCH):
        a = cols[g * CS : (g + 1) * CS, :]
        askv[:, g * CS : (g + 1) * CS] = jnp.broadcast_to(
            jnp.sum(jnp.where(eye, a, 0), axis=0, keepdims=True), (8, CS)
        )

    outs = [pltpu.make_async_copy(askv, askrow_out, out_s.at[0])]
    outs[0].start()
    drain(ug.at[1], ag_r.at[0])
    drain(ug.at[3], ag_r.at[7])
    drain(ug.at[5], ag_r.at[8])
    fetch[3].wait()

    drain(emb.at[pl.ds(1, NDEV - 1)], rp_r)
    e = jnp.dot(
        back[...], emb[...].reshape(NDEV * SLOTS, D), preferred_element_type=F32
    ).astype(BF)
    root = jnp.sqrt(F32(D))
    hid = jnp.dot(e, w_v[...], preferred_element_type=F32)
    rs = lax.rsqrt(jnp.mean(hid * hid, axis=1, keepdims=True) + epsilon)
    iv = (hid * rs / root).astype(BF)
    uf2 = ug[0].astype(F32)
    positive = jnp.sum(iv.astype(F32) * uf2, axis=1, keepdims=True) * score_scale
    drain(ug.at[7, top], ag_r.at[9])
    drain(ug.at[7, bot], ag_r.at[10])
    tot = jnp.zeros((BD, 1), F32)
    for k in range(8):
        ex = jnp.exp(nt(iv, ug[k]) * score_scale)
        tot = tot + jnp.sum(ex, axis=1, keepdims=True)
        exb[:, k * BD : (k + 1) * BD] = ex.astype(BF)
    mix = jnp.dot(exb[...], ug[...].reshape(8 * BD, D), preferred_element_type=F32)
    xent = jnp.log(tot) - positive
    cw = 1.0 / (1.0 + xent / cauchy_scale)
    dvec = cw * score_scale * (mix / tot - uf2)
    inner = jnp.sum(hid * dvec, axis=1, keepdims=True)
    dh = (rs / root * (dvec - hid * rs * rs * inner / D)).astype(BF)

    wgs[...] = tn(e, dh).astype(BF).reshape(8, 64, D)
    for k in range(4):
        send(wgs.at[k * 2 + 1 - c], wgr.at[k], wg_s.at[0], wg_r.at[0], other)

    drow = nt(dh, w_v[...]).astype(BF)
    for g in ORDER:
        part = jnp.dot(forth[g * CS : (g + 1) * CS, :], drow, preferred_element_type=F32)
        drs[g * CH : (g + 1) * CH] = part.astype(BF).reshape(CH, SLOTS, D)
        for i in chunk(g):
            send(drs.at[i], drow_out.at[i], gr_s, gr_r, at(*split(i)))
    outs.append(pltpu.make_async_copy(drs.at[0], drow_out.at[0], out_s.at[1]))
    outs[1].start()

    drain(wgr, wg_r.at[0])
    for k in range(4):
        both = wgs[k * 2 + c].astype(F32) + wgr[k].astype(F32)
        wg2[k * 16 : (k + 1) * 16] = both.astype(BF).reshape(16, 4, D)
    for j in sorted(range(1, 64), key=lambda j: -hops(j // 16 * 2 + j // 4 % 4 * 8 + j % 4 * 32)):
        xi, ze, et = j // 16, (j // 4) % 4, j % 4
        src = wg2.at[xs[xi] * 8 + zs[ze] + ys[et]]
        send(src, wg_out.at[j], wg_s.at[1], wg_r.at[1], at(xi, 0, ze, et))
    outs.append(
        pltpu.make_async_copy(wg2.at[x * 16 + z * 4 + y], wg_out.at[0], out_s.at[2])
    )
    outs[2].start()

    drain(drow_out.at[pl.ds(1, NDEV - 1)], gr_r)
    drain(wg_out.at[pl.ds(1, 63)], wg_r.at[1])

    for cp in outs:
        cp.wait()
    drain(t1.at[pl.ds(1, 7)], rq_s.at[0])
    drain(asked.at[pl.ds(1, 15)], rq_s.at[1])
    drain(ug.at[0], ag_s.at[0])
    for m in (1, 2, 3, 4, 5, 6, 9, 10):
        drain(ug.at[0, top], ag_s.at[m])
    for m in (7, 8):
        drain(ug.at[0], ag_s.at[m])
    drain(reply.at[pl.ds(1, NDEV - 1)], rp_s)
    drain(drs.at[pl.ds(1, NDEV - 1)], gr_s)
    drain(wgr, wg_s.at[0])
    drain(wg2.at[pl.ds(1, 63)], wg_s.at[1])


CUTS = (0, 128, 256, 512, 768, 1024, 1280, 1536, 1792, 2048, 2304, 2560, 2816, 3072, 3328, 3584, 3840, 4096)


def table_kernel(ask_ref, drow_ref, wg_ref, out_ref, wg_out, rows_v, wg_v, buf, sems):
    bring = pltpu.make_async_copy(wg_ref, wg_v, sems.at[0])
    bring.start()
    rows_v[...] = drow_ref[...].reshape(NDEV * SLOTS, D)
    copies = []
    for k, (lo, hi) in enumerate(zip(CUTS[:-1], CUTS[1:])):
        hit = ask_ref[0:1, :] == lax.broadcasted_iota(I32, (hi - lo, NDEV * SLOTS), 0) + lo
        mat = jnp.where(hit, F32(1), F32(0)).astype(BF)
        buf[lo:hi, :] = jnp.dot(mat, rows_v[...], preferred_element_type=F32).astype(BF)
        rows = pl.ds(lo, hi - lo)
        copies.append(pltpu.make_async_copy(buf.at[rows], out_ref.at[rows], sems.at[k + 1]))
        copies[-1].start()
        if k == 8:
            bring.wait()
            wg_out[...] = jnp.sum(wg_v[...].astype(F32), axis=0)
    for cp in copies:
        cp.wait()


def local(user_vectors, item_table, tower_weight, item_owner, item_row):
    dma = pltpu.SemaphoreType.DMA
    vm = pl.BlockSpec(memory_space=pltpu.VMEM)
    hbm = pl.BlockSpec(memory_space=pl.ANY)
    n = NDEV * SLOTS
    scratch = [
        pltpu.VMEM((BD, D), BF),
        pltpu.VMEM((D, D), BF),
        pltpu.VMEM((1, BD), I32),
        pltpu.VMEM((1, BD), I32),
        pltpu.VMEM((ROWS, D), BF),
        pltpu.VMEM((8, 1, 128), I32),
        pltpu.VMEM((8, 1, 128), I32),
        pltpu.VMEM((16, 8, 1, 128), I32),
        pltpu.VMEM((n, 128), I32),
        pltpu.VMEM((NDEV, SLOTS, D), BF),
        pltpu.VMEM((NDEV, SLOTS, D), BF),
        pltpu.VMEM((NDEV, SLOTS, D), BF),
        pltpu.VMEM((8, BD, D), BF),
        pltpu.VMEM((BD, n), BF),
        pltpu.VMEM((n, BD), BF),
        pltpu.VMEM((BD, 8 * BD), BF),
        pltpu.VMEM((n, ROWS), BF),
        pltpu.VMEM((8, 64, D), BF),
        pltpu.VMEM((4, 64, D), BF),
        pltpu.VMEM((64, 4, D), BF),
        pltpu.VMEM((8, n), I32),
        dma((3,)),
        dma((5,)),
        dma((11,)),
        dma((11,)),
        dma((2,)),
        dma((2,)),
        dma,
        dma,
        dma,
        dma,
        dma((2,)),
        dma((2,)),
    ]
    drow, ask, shares = pl.pallas_call(
        step_kernel,
        out_shape=(
            jax.ShapeDtypeStruct((NDEV, SLOTS, D), BF),
            jax.ShapeDtypeStruct((8, n), I32),
            jax.ShapeDtypeStruct((64, 4, D), BF),
        ),
        in_specs=[pl.BlockSpec(memory_space=pl.ANY)] * 5,
        out_specs=(hbm, hbm, hbm),
        scratch_shapes=scratch,
        compiler_params=pltpu.CompilerParams(
            collective_id=0, has_side_effects=True, vmem_limit_bytes=60 * 1024 * 1024
        ),
    )(user_vectors, item_table, tower_weight, item_owner.reshape(1, BD), item_row.reshape(1, BD))
    return pl.pallas_call(
        table_kernel,
        out_shape=(
            jax.ShapeDtypeStruct((ROWS, D), BF),
            jax.ShapeDtypeStruct((4, D), F32),
        ),
        in_specs=[vm, vm, hbm],
        out_specs=(hbm, vm),
        scratch_shapes=[
            pltpu.VMEM((n, D), BF),
            pltpu.VMEM((64, 4, D), BF),
            pltpu.VMEM((ROWS, D), BF),
            dma((len(CUTS),)),
        ],
    )(ask, drow, shares)


def solution(mesh):
    return jax.shard_map(
        local,
        mesh=mesh,
        in_specs=(
            P(("batch", "item"), None),
            P(("batch", "item"), None),
            P(),
            P(("batch", "item"), None),
            P(("batch", "item")),
        ),
        out_specs=(P(("batch", "item"), None), P(("batch", "item"), None)),
        check_vma=False,
    )
```
